512 devices in a mesh: member: 32 (over x, y, core), region: 16 (over z).
Axes of the slice: x: 4, y: 4, z: 16, core: 2. Of those that a mesh axis runs over, the one named last changes fastest.
Arguments:
- state_prior: bfloat16 [256, 1572864], P('member', 'region'), may hold values from -6 to 6
- obs_prior: bfloat16 [256, 131072], P('member', 'region'), may hold values from -6 to 6
- obs_value: float32 [131072], P('region'), may hold values from -12 to 12
- obs_rinv: float32 [131072], P('region'), may hold values from 0.02 to 0.3
- tile_obs: int32 [1024, 2048], P('region'), may hold values from 64 to 10175, as said below
- tile_count: int32 [1024], P('region'), may hold values from 128 to 2048, as said below
Outputs:
- analysis: bfloat16 [256, 1572864], P('member', 'region')
The draws below stay inside these ranges and needn't reach their ends.
Inputs may be any that keep to these rules, and one draw needn't show every extreme that they name: tile_obs[t] holds each widened position from i * 128 + 128 / 2 to i * 128 + 128 / 2 + 2047 exactly once, for tile i of its region. `tile_count`: each region has a tile with all 2048 slots live.
All inputs are finite; a program needn't handle non-finite values.
Results may differ from the reference program's by a relative error of at most 0.0015.
The reference program's roundings to bfloat16 on the way (of `xpert` and `wfull`) count: a program that leaves them out, or rounds other values in their place, can miss the bound.
Values may be sent and summed in bfloat16 or wider, within the bound.
No kernel may reach another device: no remote copies, remote signals or barrier semaphores. Data moves between devices by JAX's collectives and lax.ppermute only.
A program may use at most 128 MiB of HBM per device.

```python
import math
import jax
import jax.numpy as jnp
from jax import lax

MEMBERS = 256
OBS_TILE = 128
SLOTS = 2048
ITERS = 4
CELLS = 1536
NT_REG = 64
TILES = 1024
OBS_REG = 8192
OBS_ALL = 131072
RIM = 1024
LOC = 512


def draw_tile_obs(key, part):
    keys = jax.random.split(key, TILES)
    orders = jax.vmap(lambda one: jax.random.permutation(one, SLOTS))(keys).astype(jnp.int32)
    local_tile = jnp.arange(TILES, dtype=jnp.int32) % NT_REG
    start = local_tile * OBS_TILE + OBS_TILE // 2
    return (start[:, None] + orders).astype(jnp.int32)


def draw_tile_count(key, part):
    regions = TILES // NT_REG
    centers = jax.random.randint(jax.random.fold_in(key, 11), (regions,), 0, NT_REG)
    noise = jax.random.randint(jax.random.fold_in(key, 12), (TILES,), 0, SLOTS // 16)
    index = jnp.arange(TILES, dtype=jnp.int32)
    dist = jnp.abs(index % NT_REG - centers[index // NT_REG])
    value = SLOTS - SLOTS // 16 * dist + noise * (dist > 0).astype(jnp.int32)
    return jnp.clip(value, SLOTS // 16, SLOTS).astype(jnp.int32)


def block_scale(rng, dims, shards, low, top_value):
    def one(axis_at, shards_of):
        heights = jax.random.uniform(jax.random.fold_in(jax.random.fold_in(rng, 6), axis_at), (shards_of,), jnp.float32, low / len(shards), top_value / len(shards))
        return jnp.repeat(jnp.exp(heights), dims[axis_at] // shards_of).reshape((-1,) + (1,) * (len(dims) - axis_at - 1))

    level = one(*shards[0])
    for cut in shards[1:]:
        level = level * one(*cut)
    return level


def normal_values(stream_key, extent, deviation, reach, cuts=(), kind=jnp.bfloat16):
    entries = deviation * jax.random.normal(stream_key, extent, jnp.float32)
    if cuts:
        entries = entries * block_scale(stream_key, extent, cuts, -0.22, 0.18)
    return jnp.clip(entries, -reach, reach).astype(kind)


def setup_inputs(seed: int = 0) -> dict:
    seeds = jax.random.split(jax.random.key(seed), 7)
    return {
        "state_prior": normal_values(seeds[0], (MEMBERS, TILES * CELLS), 1.0, 6.0, ((0, 32), (1, 16))),
        "obs_prior": normal_values(seeds[1], (MEMBERS, OBS_ALL), 1.0, 6.0, ((0, 32), (1, 16))),
        "obs_value": normal_values(seeds[2], (OBS_ALL,), 2.0, 12.0, ((0, 16),), jnp.float32),
        "obs_rinv": jnp.clip(jnp.exp(math.log(0.3) - 2.7080503 * jax.random.uniform(seeds[3], (OBS_ALL,), jnp.float32) ** block_scale(seeds[3], (OBS_ALL,), ((0, 16),), -0.2, 0.2)), 0.02, 0.3),
        "tile_obs": draw_tile_obs(jax.random.fold_in(seeds[6], 71), 0),
        "tile_count": draw_tile_count(jax.random.fold_in(seeds[6], 71), 0),
    }


def analyse(xb, yb, yobs, rinv, slot_pos, count, center):
    size = xb.shape[0]
    slots = yb.shape[1]
    eye = jnp.eye(size, dtype=jnp.float32)
    xfull = xb.astype(jnp.float32)
    xbar = lax.optimization_barrier(jnp.mean(xfull, axis=0))
    xpert = (xfull - xbar).astype(jnp.bfloat16)
    ysel = yb.astype(jnp.float32)
    ybar = lax.optimization_barrier(jnp.mean(ysel, axis=0))
    ypert = ysel - ybar
    depart = yobs - ybar
    dist = jnp.abs(slot_pos - center).astype(jnp.float32) / LOC
    live = (jnp.arange(slots) < count).astype(jnp.float32)
    weight = live * rinv / (1.0 + dist * dist)
    cweighted = ypert * weight
    amat = (size - 1.0) * eye + jnp.dot(cweighted, ypert.T, precision=lax.Precision.HIGHEST)
    rhs = jnp.dot(cweighted, depart, precision=lax.Precision.HIGHEST)
    factor = jnp.linalg.cholesky(amat)
    inner = lax.linalg.triangular_solve(factor, rhs[:, None], left_side=True, lower=True)
    wmean = lax.linalg.triangular_solve(factor, inner, left_side=True, lower=True, transpose_a=True)[:, 0]
    mmat = amat / (size - 1.0)
    scale = jnp.sqrt(jnp.sum(mmat * mmat))
    yiter = mmat / scale
    ziter = eye
    for step in range(ITERS):
        middle = 1.5 * eye - 0.5 * jnp.dot(ziter, yiter, precision=lax.Precision.HIGHEST)
        yiter = jnp.dot(yiter, middle, precision=lax.Precision.HIGHEST)
        ziter = jnp.dot(middle, ziter, precision=lax.Precision.HIGHEST)
    wfull = (ziter / jnp.sqrt(scale) + wmean[:, None]).astype(jnp.bfloat16)
    result = xbar + jnp.dot(wfull.T.astype(jnp.float32), xpert.astype(jnp.float32), preferred_element_type=jnp.float32)
    return result.astype(jnp.bfloat16)

def reference(state_prior, obs_prior, obs_value, obs_rinv, tile_obs, tile_count):
    prior_pad = jnp.pad(obs_prior, ((0, 0), (RIM, RIM)))
    value_pad = jnp.pad(obs_value, (RIM, RIM))
    rinv_pad = jnp.pad(obs_rinv, (RIM, RIM))

    def one_tile(tile):
        region_base = tile // NT_REG * OBS_REG
        local_tile = tile % NT_REG
        slot_pos = tile_obs[tile]
        where = (slot_pos + region_base).astype(jnp.int32)
        ybl = jnp.take(prior_pad, where, axis=1)
        yobs = jnp.take(value_pad, where)
        rinv = jnp.take(rinv_pad, where)
        xb = lax.dynamic_slice_in_dim(state_prior, (tile * CELLS).astype(jnp.int32), CELLS, 1)
        center = RIM + local_tile * OBS_TILE + OBS_TILE // 2
        return analyse(xb, ybl, yobs, rinv, slot_pos, tile_count[tile], center)
    tiles_out = lax.map(one_tile, jnp.arange(TILES, dtype=jnp.int32))
    return jnp.transpose(tiles_out, (1, 0, 2)).reshape(MEMBERS, TILES * CELLS)
```

```python
import functools

import jax
import jax.numpy as jnp
from jax import lax
from jax.experimental import pallas as pl
from jax.experimental.pallas import tpu as pltpu
from jax.sharding import PartitionSpec as P

OBS_TILE = 128
ITERS = 4
RIM = 1024
LOC = 512
LANES = 128
PANEL = 32

F32 = jnp.float32
BF16 = jnp.bfloat16


def iota(shape, dim):
    return lax.broadcasted_iota(jnp.int32, shape, dim)


def dot_nt(a, b):
    return lax.dot_general(a, b, (((1,), (1,)), ((), ())), preferred_element_type=F32)


def split2(x):
    high = x.astype(BF16)
    return high, (x - high.astype(F32)).astype(BF16)


def split3(x):
    high = x.astype(BF16)
    rest = x - high.astype(F32)
    mid = rest.astype(BF16)
    return high, mid, (rest - mid.astype(F32)).astype(BF16)


def dot_three(a, b):
    ah, al = split2(a)
    bh, bl = split2(b)
    dot = functools.partial(jnp.dot, preferred_element_type=F32)
    return dot(ah, bh) + (dot(ah, bl) + dot(al, bh))


def window_kernel(before_ref, prior_ref, after_ref, out_ref, wide_ref):
    groups, members, width = out_ref.shape
    length = prior_ref.shape[1]
    wide_ref[:, :RIM] = before_ref[:members, :].astype(BF16)
    wide_ref[:, RIM : RIM + length] = prior_ref[...]
    wide_ref[:, RIM + length :] = after_ref[:members, :].astype(BF16)
    stride = length // groups
    for group in range(groups):
        out_ref[group] = wide_ref[:, group * stride : group * stride + width]


def weight_kernel(
    members, here_ref, count_ref, slot_ref, before_ref, value_ref, rinv_ref, after_ref, out_ref, wide_ref
):
    tiles = out_ref.shape[0] - 1
    width = out_ref.shape[1]
    slots = slot_ref.shape[1]
    length = value_ref.shape[1]
    for row, own in enumerate((value_ref, rinv_ref)):
        at = slice(row, row + 1)
        side = slice(members + row, members + row + 1)
        wide_ref[at, :RIM] = before_ref[side, :]
        wide_ref[at, RIM : RIM + length] = own[...]
        wide_ref[at, RIM + length :] = after_ref[side, :]
    here = here_ref[0]
    start = pl.multiple_of(here * (tiles * OBS_TILE), LANES)
    window = pl.ds(start, width)
    out_ref[tiles : tiles + 1, :] = wide_ref[0:1, window]
    rinv = wide_ref[1:2, window]
    groups = width // LANES
    padded = -(-groups // 8) * 8
    for tile in range(tiles):
        place = slot_ref[pl.ds(here * tiles + tile, 1), :] - start
        high = lax.shift_right_logical(place, 7)
        low = lax.bitwise_and(place, LANES - 1)
        live = iota((1, slots), 1) < count_ref[here * tiles + tile]
        ones_high = jnp.where((iota((padded, slots), 0) == high) & live, 1.0, 0.0).astype(BF16)
        ones_low = jnp.where(iota((LANES, slots), 0) == low, 1.0, 0.0).astype(BF16)
        mask = dot_nt(ones_high, ones_low)
        center = RIM + tile * OBS_TILE + OBS_TILE // 2
        for group in range(groups):
            at = slice(group * LANES, (group + 1) * LANES)
            position = iota((1, LANES), 1) + group * LANES
            dist = jnp.abs(position - center).astype(F32) / LOC
            out_ref[tile : tile + 1, at] = (
                mask[group : group + 1, :] * rinv[:, at] / (1.0 + dist * dist)
            )


def gram(y_ref, w_ref, amat, rhs):
    size, width = y_ref.shape
    tiles = amat.shape[0]
    chunk = 256
    shift = [jnp.zeros((size, LANES), F32) for _ in range(tiles)]
    right = [jnp.zeros((8, size), F32) for _ in range(tiles)]
    offset = [jnp.zeros((1, chunk), F32) for _ in range(tiles)]
    for step in range(width // chunk):
        at = slice(step * chunk, (step + 1) * chunk)
        yb = y_ref[:, at]
        yf = yb.astype(F32)
        ybar = jnp.sum(yf, axis=0, keepdims=True) * (1.0 / size)
        pert = yf - ybar
        depart = w_ref[tiles : tiles + 1, at] - ybar
        for tile in range(tiles):
            weight = w_ref[tile : tile + 1, at]
            cweighted = pert * weight
            parts = split3(cweighted)
            product = dot_nt(parts[0], yb) + (dot_nt(parts[1], yb) + dot_nt(parts[2], yb))
            if step == 0:
                amat[tile] = product
            else:
                amat[tile] += product
            scaled = cweighted * ybar
            shift[tile] += scaled[:, :LANES] + scaled[:, LANES:]
            drive = weight * depart
            rows = iota((8, chunk), 0)
            dh, dm, dl = split3(drive)
            stacked = jnp.where(
                rows == 0,
                dh.astype(F32),
                jnp.where(rows == 1, dm.astype(F32), jnp.where(rows == 2, dl.astype(F32), 0.0)),
            ).astype(BF16)
            right[tile] += dot_nt(stacked, yb)
            offset[tile] += drive * ybar
    diagonal = iota((size, size), 0) == iota((size, size), 1)
    for tile in range(tiles):
        row = jnp.sum(shift[tile], axis=1, keepdims=True)
        amat[tile] += jnp.where(diagonal, size - 1.0, 0.0) - row
        total = jnp.sum(right[tile], axis=0, keepdims=True)
        rhs[tile] = total - jnp.sum(offset[tile], axis=1, keepdims=True)


def sweep_panel(amat, rhs, tile, panel):
    size = amat.shape[1]
    base = pl.multiple_of(panel * PANEL, PANEL)
    rows = pl.ds(base, PANEL)
    ngroup = PANEL // 8
    lane = iota((8, LANES), 1)
    sub = iota((8, LANES), 0)
    wide = iota((1, size), 1)
    old = amat[tile, rows, :]
    low = [old[8 * g : 8 * g + 8, :LANES] for g in range(ngroup)]
    high = [old[8 * g : 8 * g + 8, LANES:] for g in range(ngroup)]
    line = rhs[tile]
    place = iota((PANEL, size), 1) - iota((PANEL, size), 0)
    brep = jnp.sum(jnp.where(place == base, line, 0.0), axis=1, keepdims=True)
    upper = base >= LANES
    within = jnp.where(upper, base - LANES, base)
    for block in range(ngroup):
        half = [jnp.where(upper, high[g], low[g]) for g in range(ngroup)]
        cols = []
        for c in range(8):
            pick = lane == within + (8 * block + c)
            cols.append(
                [
                    jnp.broadcast_to(
                        jnp.sum(jnp.where(pick, half[g], 0.0), axis=1, keepdims=True), (8, LANES)
                    )
                    for g in range(ngroup)
                ]
            )
        for j in range(8):
            at = base + (8 * block + j)
            pivot = jnp.broadcast_to(cols[j][block][j : j + 1, :], (8, LANES))
            inverse = 1.0 / pivot
            here = sub == j
            scale = [-(cols[j][g] * inverse) for g in range(ngroup)]
            scale[block] = jnp.where(here, inverse, scale[block])
            line_low = jnp.broadcast_to(low[block][j : j + 1, :], (8, LANES))
            line_high = jnp.broadcast_to(high[block][j : j + 1, :], (8, LANES))
            mask_low, mask_high = lane == at, lane + LANES == at
            for g in range(ngroup):
                first, second = low[g], high[g]
                if g == block:
                    first, second = jnp.where(here, 0.0, first), jnp.where(here, 0.0, second)
                low[g] = jnp.where(mask_low, scale[g], first + scale[g] * line_low)
                high[g] = jnp.where(mask_high, scale[g], second + scale[g] * line_high)
            for c in range(j + 1, 8):
                entry = jnp.broadcast_to(cols[c][block][j : j + 1, :], (8, LANES))
                for g in range(ngroup):
                    kept = jnp.where(here, 0.0, cols[c][g]) if g == block else cols[c][g]
                    cols[c][g] = kept + scale[g] * entry
    new = jnp.concatenate(
        [jnp.concatenate(low, axis=0), jnp.concatenate(high, axis=0)], axis=1
    )
    colsum = jnp.sum(new * brep, axis=0, keepdims=True)
    inside = (wide >= base) & (wide < base + PANEL)
    swept = wide < base
    rhs[tile] = jnp.where(inside, 0.0, line) - jnp.where(swept | inside, -colsum, colsum)
    signed = jnp.where(inside, 0.0, jnp.where(swept, -old, old))
    update = lax.dot_general(
        signed,
        new,
        (((0,), (0,)), ((), ())),
        precision=lax.Precision.HIGHEST,
        preferred_element_type=F32,
    )
    amat[tile] = jnp.where(inside, 0.0, amat[tile]) - update
    amat[tile, rows, :] = new


def solve_kernel(y_ref, w_ref, out_ref, amat, rhs, ymat, zmat):
    tiles, size = amat.shape[0], amat.shape[1]
    gram(y_ref, w_ref, amat, rhs)
    eye = jnp.where(iota((size, size), 0) == iota((size, size), 1), 1.0, 0.0).astype(F32)
    root = []
    for tile in range(tiles):
        mmat = amat[tile] * (1.0 / (size - 1.0))
        squares = jnp.sum(mmat * mmat, axis=0, keepdims=True)
        scale = jnp.sqrt(jnp.sum(squares, axis=1, keepdims=True))
        root.append(lax.rsqrt(scale))
        ymat[tile] = mmat / scale
        zmat[tile] = eye
    panels = size // PANEL
    per = panels // ITERS

    def step(i, carry):
        diagonal = iota((size, size), 0) == iota((size, size), 1)
        for tile in range(tiles):
            y, z = ymat[tile], zmat[tile]
            middle = jnp.where(diagonal, 1.5, 0.0) - 0.5 * dot_three(z, y)
            ymat[tile] = dot_three(y, middle)
            zmat[tile] = dot_three(middle, z)
        for j in range(per):
            for tile in range(tiles):
                sweep_panel(amat, rhs, tile, i * per + j)
        return carry

    lax.fori_loop(0, ITERS, step, 0)
    for tile in range(tiles):
        out_ref[tile] = (zmat[tile] * root[tile] + rhs[tile]).astype(BF16)


def apply_kernel(x_ref, w_ref, out_ref):
    size, columns = x_ref.shape
    tiles = w_ref.shape[0]
    block = 512
    each = columns // tiles // block
    for step in range(columns // block):
        at = slice(step * block, (step + 1) * block)
        xfull = x_ref[:, at].astype(F32)
        xbar = jnp.sum(xfull, axis=0, keepdims=True) * (1.0 / size)
        xpert = (xfull - xbar).astype(BF16)
        moved = jnp.dot(w_ref[step // each], xpert, preferred_element_type=F32)
        out_ref[:, at] = (xbar + moved).astype(BF16)


VMEM = pl.BlockSpec(memory_space=pltpu.VMEM)
SMEM = pl.BlockSpec(memory_space=pltpu.SMEM)


def windows(before, prior, after, groups, width):
    members, length = prior.shape
    return pl.pallas_call(
        window_kernel,
        out_shape=jax.ShapeDtypeStruct((groups, members, width), BF16),
        in_specs=[VMEM] * 3,
        out_specs=VMEM,
        scratch_shapes=[pltpu.VMEM((members, length + 2 * RIM), BF16)],
        name="windows",
    )(before, prior, after)


def tile_weights(here, counts, slots, before, values, rinv, after, tiles, width):
    members = before.shape[0] - 2
    return pl.pallas_call(
        functools.partial(weight_kernel, members),
        out_shape=jax.ShapeDtypeStruct((tiles + 1, width), F32),
        in_specs=[SMEM, SMEM] + [VMEM] * 5,
        out_specs=VMEM,
        scratch_shapes=[pltpu.VMEM((8, values.shape[1] + 2 * RIM), F32)],
        cost_estimate=pl.CostEstimate(flops=50_000_000, bytes_accessed=1 << 20, transcendentals=0),
        name="tile_weights",
    )(here, counts, slots, before, values, rinv, after)


def tile_transform(y, sides):
    size, tiles = y.shape[0], sides.shape[0] - 1
    square = pltpu.VMEM((tiles, size, size), F32)
    return pl.pallas_call(
        solve_kernel,
        out_shape=jax.ShapeDtypeStruct((tiles, size, size), BF16),
        in_specs=[VMEM, VMEM],
        out_specs=VMEM,
        scratch_shapes=[square, pltpu.VMEM((tiles, 1, size), F32), square, square],
        compiler_params=pltpu.CompilerParams(vmem_limit_bytes=32 << 20),
        cost_estimate=pl.CostEstimate(
            flops=2 * 9 * tiles * size * size * size * 6, bytes_accessed=8 << 20, transcendentals=0
        ),
        name="tile_transform",
    )(y, sides)


def tile_apply(states, transform):
    size, columns = states.shape
    return pl.pallas_call(
        apply_kernel,
        out_shape=jax.ShapeDtypeStruct((size, columns), BF16),
        in_specs=[VMEM, VMEM],
        out_specs=VMEM,
        compiler_params=pltpu.CompilerParams(vmem_limit_bytes=32 << 20),
        cost_estimate=pl.CostEstimate(
            flops=2 * size * size * columns, bytes_accessed=4 * size * columns, transcendentals=0
        ),
        name="tile_apply",
    )(states, transform)


def edges(value, width):
    size = lax.axis_size("region")
    up = [(i, i + 1) for i in range(size - 1)]
    down = [(i + 1, i) for i in range(size - 1)]
    length = value.shape[1]
    before = lax.ppermute(value[:, length - width :], "region", up)
    after = lax.ppermute(value[:, :width], "region", down)
    return before, after


def body(state_prior, obs_prior, obs_value, obs_rinv, tile_obs, tile_count):
    members_here = state_prior.shape[0]
    groups = lax.axis_size("member")
    here = lax.axis_index("member")
    tiles_region, slots = tile_obs.shape
    per_dev = tiles_region // groups
    cells = state_prior.shape[1] // tiles_region
    columns = per_dev * cells
    stride = per_dev * OBS_TILE
    span = slots + stride
    width = -(-span // 256) * 256

    sending = state_prior.reshape(members_here, groups, columns).transpose(1, 0, 2)

    stacked = jnp.concatenate(
        [obs_prior.astype(F32), obs_value[None, :], obs_rinv[None, :]], axis=0
    )
    before, after = edges(stacked, RIM)
    sent = windows(before, obs_prior, after, groups, width)
    yall = lax.all_to_all(sent, "member", split_axis=0, concat_axis=0, tiled=True)
    yall = yall.reshape(groups * members_here, width)
    states = lax.all_to_all(sending, "member", split_axis=0, concat_axis=0, tiled=True)
    states = states.reshape(groups * members_here, columns)
    sides = tile_weights(
        here[None], tile_count, tile_obs, before, obs_value[None], obs_rinv[None], after, per_dev, width
    )
    transform = tile_transform(yall, sides)
    updated = tile_apply(states, transform)
    returned = lax.all_to_all(
        updated.reshape(groups, members_here, columns),
        "member",
        split_axis=0,
        concat_axis=0,
        tiled=True,
    )
    return returned.transpose(1, 0, 2).reshape(members_here, tiles_region * cells)


def solution(mesh):
    placed = (
        P("member", "region"),
        P("member", "region"),
        P("region"),
        P("region"),
        P("region", None),
        P("region"),
    )
    return jax.shard_map(
        body, mesh=mesh, in_specs=placed, out_specs=P("member", "region"), check_vma=False
    )
```

```python
import functools

import jax
import jax.numpy as jnp
from jax import lax
from jax.experimental import pallas as pl
from jax.experimental.pallas import tpu as pltpu
from jax.sharding import PartitionSpec as P

OBS_TILE = 128
ITERS = 4
RIM = 1024
LOC = 512
LANES = 128
PANEL = 32

F32 = jnp.float32
BF16 = jnp.bfloat16


def iota(shape, dim):
    return lax.broadcasted_iota(jnp.int32, shape, dim)


def dot_nt(a, b):
    return lax.dot_general(a, b, (((1,), (1,)), ((), ())), preferred_element_type=F32)


def split2(x):
    high = x.astype(BF16)
    return high, (x - high.astype(F32)).astype(BF16)


def split3(x):
    high = x.astype(BF16)
    rest = x - high.astype(F32)
    mid = rest.astype(BF16)
    return high, mid, (rest - mid.astype(F32)).astype(BF16)


def dot_three(a, b):
    ah, al = split2(a)
    bh, bl = split2(b)
    return jnp.dot(
        jnp.concatenate([ah, ah, al], axis=1),
        jnp.concatenate([bh, bl, bh], axis=0),
        preferred_element_type=F32,
    )


def dot_tn_six(a, b):
    ah, am, al = split3(a)
    bh, bm, bl = split3(b)
    left = jnp.concatenate([ah, ah, am, am, ah, al], axis=0)
    right = jnp.concatenate([bh, bm, bh, bm, bl, bh], axis=0)
    return lax.dot_general(left, right, (((0,), (0,)), ((), ())), preferred_element_type=F32)


def edge_kernel(prior_ref, value_ref, rinv_ref, last_ref, first_ref):
    members, length = prior_ref.shape
    for out, start in ((last_ref, length - RIM), (first_ref, 0)):
        at = slice(start, start + RIM)
        out[:members, :] = prior_ref[:, at].astype(F32)
        out[members : members + 1, :] = value_ref[:, at]
        out[members + 1 : members + 2, :] = rinv_ref[:, at]


def window_kernel(before_ref, prior_ref, after_ref, out_ref, wide_ref):
    groups, members, width = out_ref.shape
    length = prior_ref.shape[1]
    wide_ref[:, :RIM] = before_ref[:members, :].astype(BF16)
    wide_ref[:, RIM : RIM + length] = prior_ref[...]
    wide_ref[:, RIM + length :] = after_ref[:members, :].astype(BF16)
    stride = length // groups
    for group in range(groups):
        out_ref[group] = wide_ref[:, group * stride : group * stride + width]


def weight_kernel(
    members, here_ref, count_ref, slot_ref, before_ref, value_ref, rinv_ref, after_ref, out_ref, wide_ref
):
    tiles = out_ref.shape[0] - 1
    width = out_ref.shape[1]
    slots = slot_ref.shape[1]
    length = value_ref.shape[1]
    for row, own in enumerate((value_ref, rinv_ref)):
        at = slice(row, row + 1)
        side = slice(members + row, members + row + 1)
        wide_ref[at, :RIM] = before_ref[side, :]
        wide_ref[at, RIM : RIM + length] = own[...]
        wide_ref[at, RIM + length :] = after_ref[side, :]
    here = here_ref[0]
    start = pl.multiple_of(here * (tiles * OBS_TILE), LANES)
    window = pl.ds(start, width)
    out_ref[tiles : tiles + 1, :] = wide_ref[0:1, window]
    rinv = wide_ref[1:2, window]
    groups = width // LANES
    padded = -(-groups // 8) * 8
    for tile in range(tiles):
        place = slot_ref[pl.ds(here * tiles + tile, 1), :] - start
        high = lax.shift_right_logical(place, 7)
        low = lax.bitwise_and(place, LANES - 1)
        live = iota((1, slots), 1) < count_ref[here * tiles + tile]
        ones_high = jnp.where((iota((padded, slots), 0) == high) & live, 1.0, 0.0).astype(BF16)
        ones_low = jnp.where(iota((LANES, slots), 0) == low, 1.0, 0.0).astype(BF16)
        mask = dot_nt(ones_high, ones_low)
        center = RIM + tile * OBS_TILE + OBS_TILE // 2
        for group in range(groups):
            at = slice(group * LANES, (group + 1) * LANES)
            position = iota((1, LANES), 1) + group * LANES
            dist = jnp.abs(position - center).astype(F32) / LOC
            out_ref[tile : tile + 1, at] = (
                mask[group : group + 1, :] * rinv[:, at] / (1.0 + dist * dist)
            )


def gram(y_ref, w_ref, amat, rhs):
    size, width = y_ref.shape
    tiles = amat.shape[0]
    chunk = 256
    shift = [jnp.zeros((size, LANES), F32) for _ in range(tiles)]
    right = [jnp.zeros((8, size), F32) for _ in range(tiles)]
    offset = [jnp.zeros((1, chunk), F32) for _ in range(tiles)]
    for step in range(width // chunk):
        at = slice(step * chunk, (step + 1) * chunk)
        yb = y_ref[:, at]
        yf = yb.astype(F32)
        ybar = jnp.sum(yf, axis=0, keepdims=True) * (1.0 / size)
        pert = yf - ybar
        depart = w_ref[tiles : tiles + 1, at] - ybar
        for tile in range(tiles):
            weight = w_ref[tile : tile + 1, at]
            cweighted = pert * weight
            parts = split3(cweighted)
            product = dot_nt(parts[0], yb) + (dot_nt(parts[1], yb) + dot_nt(parts[2], yb))
            if step == 0:
                amat[tile] = product
            else:
                amat[tile] += product
            scaled = cweighted * ybar
            shift[tile] += scaled[:, :LANES] + scaled[:, LANES:]
            drive = weight * depart
            rows = iota((8, chunk), 0)
            dh, dm, dl = split3(drive)
            stacked = jnp.where(
                rows == 0,
                dh.astype(F32),
                jnp.where(rows == 1, dm.astype(F32), jnp.where(rows == 2, dl.astype(F32), 0.0)),
            ).astype(BF16)
            right[tile] += dot_nt(stacked, yb)
            offset[tile] += drive * ybar
    diagonal = iota((size, size), 0) == iota((size, size), 1)
    for tile in range(tiles):
        row = jnp.sum(shift[tile], axis=1, keepdims=True)
        amat[tile] += jnp.where(diagonal, size - 1.0, 0.0) - row
        total = jnp.sum(right[tile], axis=0, keepdims=True)
        rhs[tile] = total - jnp.sum(offset[tile], axis=1, keepdims=True)


def lane_copy(value, lane):
    return jnp.broadcast_to(value[:, lane : lane + 1], (8, LANES))


def row_copy(value, row):
    return jnp.broadcast_to(value[row : row + 1, :], (8, LANES))


def eliminate(amat, tile, line, solved):
    size = amat.shape[1]
    ngroup = PANEL // 8
    halves = size // LANES
    sub = iota((8, LANES), 0)
    lane = iota((8, LANES), 1)
    line = [line[:, LANES * h : LANES * h + LANES] for h in range(halves)]
    reduced = []
    for base in range(0, size, PANEL):
        first = base // LANES
        within = base % LANES
        live = range(first, halves)
        old = {
            h: amat[tile, base : base + PANEL, LANES * h : LANES * h + LANES] for h in live
        }
        part = {h: [old[h][8 * g : 8 * g + 8, :] for g in range(ngroup)] for h in live}
        right = [
            jnp.broadcast_to(
                jnp.sum(
                    jnp.where(lane - sub == within + 8 * g, line[first], 0.0), axis=1, keepdims=True
                ),
                (8, LANES),
            )
            for g in range(ngroup)
        ]
        before = list(right)
        for block in range(ngroup):
            cols = [
                [lane_copy(part[first][g], within + 8 * block + c) for c in range(8)]
                for g in range(ngroup)
            ]
            own = cols[block]
            for j in range(8):
                inverse = 1.0 / row_copy(own[j], j)
                here = sub == j
                scale = jnp.where(here, inverse, -(own[j] * inverse))

                def step(value):
                    return jnp.where(here, 0.0, value) + scale * row_copy(value, j)

                for c in range(j + 1, 8):
                    own[c] = step(own[c])
                for h in live:
                    part[h][block] = step(part[h][block])
                right[block] = step(right[block])
                yield
            for c in range(8):
                lines = {h: row_copy(part[h][block], c) for h in live}
                entry = row_copy(right[block], c)
                for g in range(ngroup):
                    if g != block:
                        for h in live:
                            part[h][g] = part[h][g] - cols[g][c] * lines[h]
                        right[g] = right[g] - cols[g][c] * entry
            yield
        reduced.append(right)
        new = {h: jnp.concatenate(part[h], axis=0) for h in live}
        for h in live:
            amat[tile, base : base + PANEL, LANES * h : LANES * h + LANES] = new[h]
        after = base + PANEL
        if after < size:
            given = jnp.concatenate(before, axis=0)
            for h in live:
                line[h] = line[h] - jnp.sum(new[h] * given, axis=0, keepdims=True)
            use = range(after // LANES, halves)
            start = use[0] * LANES
            update = dot_tn_six(
                jnp.concatenate([old[h] for h in use], axis=1),
                jnp.concatenate([new[h] for h in use], axis=1),
            )
            amat[tile, after:, start:] -= update[after - start :, :]
            yield
    solution_line = [jnp.zeros((1, LANES), F32) for _ in range(halves)]
    for base in reversed(range(0, size, PANEL)):
        first = base // LANES
        within = base % LANES
        right = reduced[base // PANEL]
        if base + PANEL < size:
            total = None
            for h in range((base + PANEL) // LANES, halves):
                term = amat[tile, base : base + PANEL, LANES * h : LANES * h + LANES] * solution_line[h]
                total = term if total is None else total + term
            known = jnp.sum(total, axis=1, keepdims=True)
            right = [right[g] - known[8 * g : 8 * g + 8, :] for g in range(ngroup)]
        placed = None
        for g in range(ngroup):
            term = jnp.where(lane - sub == within + 8 * g, right[g], 0.0)
            placed = term if placed is None else placed + term
        solution_line[first] = solution_line[first] + jnp.sum(placed, axis=0, keepdims=True)
        yield
    solved[tile] = jnp.concatenate(solution_line, axis=1)


def newton_schulz(tile, mmat, scale, zmat):
    size = mmat.shape[0]
    diagonal = iota((size, size), 0) == iota((size, size), 1)
    y = mmat / scale
    z = None
    for step in range(ITERS):
        product = y if z is None else dot_three(z, y)
        yield
        middle = jnp.where(diagonal, 1.5, 0.0) - 0.5 * product
        if step < ITERS - 1:
            y = dot_three(y, middle)
            yield
        z = middle if z is None else dot_three(middle, z)
        yield
    zmat[tile] = z * lax.rsqrt(scale)


def solve_kernel(y_ref, w_ref, out_ref, amat, rhs, zmat):
    tiles, size = amat.shape[0], amat.shape[1]
    gram(y_ref, w_ref, amat, rhs)
    solving, taking = [], []
    for tile in range(tiles):
        mmat = amat[tile] * (1.0 / (size - 1.0))
        squares = jnp.sum(mmat * mmat, axis=0, keepdims=True)
        scale = jnp.sqrt(jnp.sum(squares, axis=1, keepdims=True))
        taking.append(newton_schulz(tile, mmat, scale, zmat))
        solving.append(eliminate(amat, tile, rhs[tile], rhs))
    for work in taking:
        next(work)
    count = 0
    while solving or taking:
        solving = [work for work in solving if next(work, True) is None]
        if count % 12 == 0 or not solving:
            taking = [work for work in taking if next(work, True) is None]
        count += 1
    for tile in range(tiles):
        out_ref[tile] = (zmat[tile] + rhs[tile]).astype(BF16)


def apply_kernel(x_ref, w_ref, out_ref):
    size, columns = x_ref.shape
    tiles = w_ref.shape[0]
    block = 512
    each = columns // tiles // block
    for step in range(columns // block):
        at = slice(step * block, (step + 1) * block)
        xfull = x_ref[:, at].astype(F32)
        xbar = jnp.sum(xfull, axis=0, keepdims=True) * (1.0 / size)
        xpert = (xfull - xbar).astype(BF16)
        moved = jnp.dot(w_ref[step // each], xpert, preferred_element_type=F32)
        out_ref[:, at] = (xbar + moved).astype(BF16)


VMEM = pl.BlockSpec(memory_space=pltpu.VMEM)
SMEM = pl.BlockSpec(memory_space=pltpu.SMEM)


def windows(before, prior, after, groups, width):
    members, length = prior.shape
    return pl.pallas_call(
        window_kernel,
        out_shape=jax.ShapeDtypeStruct((groups, members, width), BF16),
        in_specs=[VMEM] * 3,
        out_specs=VMEM,
        scratch_shapes=[pltpu.VMEM((members, length + 2 * RIM), BF16)],
        compiler_params=pltpu.CompilerParams(vmem_limit_bytes=8 << 20),
        name="windows",
    )(before, prior, after)


def tile_weights(here, counts, slots, before, values, rinv, after, tiles, width):
    members = before.shape[0] - 2
    return pl.pallas_call(
        functools.partial(weight_kernel, members),
        out_shape=jax.ShapeDtypeStruct((tiles + 1, width), F32),
        in_specs=[SMEM, SMEM] + [VMEM] * 5,
        out_specs=VMEM,
        scratch_shapes=[pltpu.VMEM((8, values.shape[1] + 2 * RIM), F32)],
        compiler_params=pltpu.CompilerParams(vmem_limit_bytes=8 << 20),
        cost_estimate=pl.CostEstimate(flops=50_000_000, bytes_accessed=1 << 20, transcendentals=0),
        name="tile_weights",
    )(here, counts, slots, before, values, rinv, after)


def tile_transform(y, sides):
    size, tiles = y.shape[0], sides.shape[0] - 1
    square = pltpu.VMEM((tiles, size, size), F32)
    return pl.pallas_call(
        solve_kernel,
        out_shape=jax.ShapeDtypeStruct((tiles, size, size), BF16),
        in_specs=[VMEM, VMEM],
        out_specs=VMEM,
        scratch_shapes=[square, pltpu.VMEM((tiles, 1, size), F32), square],
        compiler_params=pltpu.CompilerParams(vmem_limit_bytes=32 << 20),
        cost_estimate=pl.CostEstimate(
            flops=2 * 9 * tiles * size * size * size * 6, bytes_accessed=8 << 20, transcendentals=0
        ),
        name="tile_transform",
    )(y, sides)


def tile_apply(states, transform):
    size, columns = states.shape
    return pl.pallas_call(
        apply_kernel,
        out_shape=jax.ShapeDtypeStruct((size, columns), BF16),
        in_specs=[VMEM, VMEM],
        out_specs=VMEM,
        compiler_params=pltpu.CompilerParams(vmem_limit_bytes=32 << 20),
        cost_estimate=pl.CostEstimate(
            flops=2 * size * size * columns, bytes_accessed=4 * size * columns, transcendentals=0
        ),
        name="tile_apply",
    )(states, transform)


def edges(prior, values, rinv):
    size = lax.axis_size("region")
    up = [(i, i + 1) for i in range(size - 1)]
    down = [(i + 1, i) for i in range(size - 1)]
    shape = jax.ShapeDtypeStruct((prior.shape[0] + 2, RIM), F32)
    last, first = pl.pallas_call(
        edge_kernel,
        out_shape=(shape, shape),
        in_specs=[VMEM] * 3,
        out_specs=(VMEM, VMEM),
        compiler_params=pltpu.CompilerParams(vmem_limit_bytes=4 << 20),
        name="edges",
    )(prior, values, rinv)
    before = lax.ppermute(last, "region", up)
    after = lax.ppermute(first, "region", down)
    return before, after


def body(state_prior, obs_prior, obs_value, obs_rinv, tile_obs, tile_count):
    members_here = state_prior.shape[0]
    groups = lax.axis_size("member")
    here = lax.axis_index("member")
    tiles_region, slots = tile_obs.shape
    per_dev = tiles_region // groups
    cells = state_prior.shape[1] // tiles_region
    columns = per_dev * cells
    stride = per_dev * OBS_TILE
    span = slots + stride
    width = -(-span // 256) * 256

    sending = state_prior.reshape(members_here, groups, columns).transpose(1, 0, 2)

    before, after = edges(obs_prior, obs_value[None], obs_rinv[None])
    sent = windows(before, obs_prior, after, groups, width)
    yall = lax.all_to_all(sent, "member", split_axis=0, concat_axis=0, tiled=True)
    yall = yall.reshape(groups * members_here, width)
    sides = tile_weights(
        here[None], tile_count, tile_obs, before, obs_value[None], obs_rinv[None], after, per_dev, width
    )
    sending, sides = lax.optimization_barrier((sending, sides))
    states = lax.all_to_all(sending, "member", split_axis=0, concat_axis=0, tiled=True)
    states = states.reshape(groups * members_here, columns)
    transform = tile_transform(yall, sides)
    updated = tile_apply(states, transform)
    returned = lax.all_to_all(
        updated.reshape(groups, members_here, columns),
        "member",
        split_axis=0,
        concat_axis=0,
        tiled=True,
    )
    return returned.transpose(1, 0, 2).reshape(members_here, tiles_region * cells)


def solution(mesh):
    placed = (
        P("member", "region"),
        P("member", "region"),
        P("region"),
        P("region"),
        P("region", None),
        P("region"),
    )
    return jax.shard_map(
        body, mesh=mesh, in_specs=placed, out_specs=P("member", "region"), check_vma=False
    )
```

```python
import functools

import jax
import jax.numpy as jnp
from jax import lax
from jax.experimental import pallas as pl
from jax.experimental.pallas import tpu as pltpu
from jax.sharding import PartitionSpec as P

OBS_TILE = 128
ITERS = 4
RIM = 1024
LOC = 512
LANES = 128
PANEL = 32

F32 = jnp.float32
BF16 = jnp.bfloat16


def iota(shape, dim):
    return lax.broadcasted_iota(jnp.int32, shape, dim)


def dot_nt(a, b):
    return lax.dot_general(a, b, (((1,), (1,)), ((), ())), preferred_element_type=F32)


def split2(x):
    high = x.astype(BF16)
    return high, (x - high.astype(F32)).astype(BF16)


def split3(x):
    high = x.astype(BF16)
    rest = x - high.astype(F32)
    mid = rest.astype(BF16)
    return high, mid, (rest - mid.astype(F32)).astype(BF16)


def dot_three(a, b):
    ah, al = split2(a)
    bh, bl = split2(b)
    return jnp.dot(
        jnp.concatenate([ah, ah, al], axis=1),
        jnp.concatenate([bh, bl, bh], axis=0),
        preferred_element_type=F32,
    )


def dot_tn_six(a, b):
    ah, am, al = split3(a)
    bh, bm, bl = split3(b)
    left = jnp.concatenate([ah, ah, am, am, ah, al], axis=0)
    right = jnp.concatenate([bh, bm, bh, bm, bl, bh], axis=0)
    return lax.dot_general(left, right, (((0,), (0,)), ((), ())), preferred_element_type=F32)


def edge_kernel(prior_ref, value_ref, rinv_ref, last_ref, first_ref, held_ref, sems):
    members, length = prior_ref.shape
    copies = [pltpu.make_async_copy(prior_ref, held_ref, sems.at[0])]
    for side, (out, start) in enumerate(((last_ref, length - RIM), (first_ref, 0))):
        for row, source in enumerate((value_ref, rinv_ref)):
            copies.append(
                pltpu.make_async_copy(
                    source.at[:, start : start + RIM],
                    out.at[members + row : members + row + 1, :],
                    sems.at[1 + 2 * side + row],
                )
            )
    for copy in copies:
        copy.start()
    for copy in copies:
        copy.wait()
    last_ref[:members, :] = held_ref[:, length - RIM :].astype(F32)
    first_ref[:members, :] = held_ref[:, :RIM].astype(F32)


def window_kernel(before_ref, prior_ref, after_ref, out_ref):
    groups, members, half = out_ref.shape
    length = prior_ref.shape[1]
    stride = 2 * length // groups
    pieces = (
        (0, RIM, before_ref),
        (RIM, RIM + length, prior_ref),
        (RIM + length, length + 2 * RIM, after_ref),
    )
    for group in range(groups):
        start = group // 2 * stride + group % 2 * half
        for low, high, source in pieces:
            left, right = max(start, low), min(start + half, high)
            if left < right:
                out_ref[group, :, left - start : right - start] = source[
                    :members, left - low : right - low
                ].astype(BF16)


def weight_kernel(
    members, here_ref, count_ref, slot_ref, before_ref, value_ref, rinv_ref, after_ref, out_ref, wide_ref
):
    tiles = out_ref.shape[0] - 1
    width = out_ref.shape[1]
    half = width // 2
    slots = slot_ref.shape[1]
    length = value_ref.shape[1]
    for row, own in enumerate((value_ref, rinv_ref)):
        at = slice(row, row + 1)
        side = slice(members + row, members + row + 1)
        wide_ref[at, :RIM] = before_ref[side, :]
        wide_ref[at, RIM : RIM + length] = own[...]
        wide_ref[at, RIM + length :] = after_ref[side, :]
    here = here_ref[0]
    chip, core = lax.shift_right_logical(here, 1), lax.bitwise_and(here, 1)
    start = chip * (2 * tiles * OBS_TILE)
    shift = core * half
    own = pl.ds(pl.multiple_of(start + shift, LANES), half)
    other = pl.ds(pl.multiple_of(start + half - shift, LANES), half)
    out_ref[tiles : tiles + 1, :half] = wide_ref[0:1, own]
    out_ref[tiles : tiles + 1, half:] = wide_ref[0:1, other]
    rinv = (wide_ref[1:2, own], wide_ref[1:2, other])
    groups = width // LANES
    padded = -(-groups // 8) * 8
    for tile in range(tiles):
        place = slot_ref[pl.ds(here * tiles + tile, 1), :] - (start + shift)
        place = jnp.where(place < 0, place + width, place)
        high = lax.shift_right_logical(place, 7)
        low = lax.bitwise_and(place, LANES - 1)
        live = iota((1, slots), 1) < count_ref[here * tiles + tile]
        ones_high = jnp.where((iota((padded, slots), 0) == high) & live, 1.0, 0.0).astype(BF16)
        ones_low = jnp.where(iota((LANES, slots), 0) == low, 1.0, 0.0).astype(BF16)
        mask = dot_nt(ones_high, ones_low)
        center = RIM + core * (tiles * OBS_TILE) + tile * OBS_TILE + OBS_TILE // 2
        for group in range(groups):
            at = slice(group * LANES, (group + 1) * LANES)
            first = group * LANES // half
            begin = group * LANES - first * half
            position = iota((1, LANES), 1) + begin
            position += half - shift if first else shift
            dist = jnp.abs(position - center).astype(F32) / LOC
            out_ref[tile : tile + 1, at] = (
                mask[group : group + 1, :]
                * rinv[first][:, begin : begin + LANES]
                / (1.0 + dist * dist)
            )


def gram(y_refs, w_ref, amat, rhs):
    size, half = y_refs[0].shape
    width = w_ref.shape[1]
    tiles = amat.shape[0]
    chunk = 256
    shift = [jnp.zeros((size, LANES), F32) for _ in range(tiles)]
    right = [jnp.zeros((8, size), F32) for _ in range(tiles)]
    offset = [jnp.zeros((1, chunk), F32) for _ in range(tiles)]
    for step in range(width // chunk):
        at = slice(step * chunk, (step + 1) * chunk)
        begin = step * chunk % half
        yb = y_refs[step * chunk // half][:, begin : begin + chunk]
        yf = yb.astype(F32)
        ybar = jnp.sum(yf, axis=0, keepdims=True) * (1.0 / size)
        pert = yf - ybar
        depart = w_ref[tiles : tiles + 1, at] - ybar
        for tile in range(tiles):
            weight = w_ref[tile : tile + 1, at]
            cweighted = pert * weight
            parts = split3(cweighted)
            product = dot_nt(parts[0], yb) + (dot_nt(parts[1], yb) + dot_nt(parts[2], yb))
            if step == 0:
                amat[tile] = product
            else:
                amat[tile] += product
            scaled = cweighted * ybar
            shift[tile] += scaled[:, :LANES] + scaled[:, LANES:]
            drive = weight * depart
            rows = iota((8, chunk), 0)
            dh, dm, dl = split3(drive)
            stacked = jnp.where(
                rows == 0,
                dh.astype(F32),
                jnp.where(rows == 1, dm.astype(F32), jnp.where(rows == 2, dl.astype(F32), 0.0)),
            ).astype(BF16)
            right[tile] += dot_nt(stacked, yb)
            offset[tile] += drive * ybar
    diagonal = iota((size, size), 0) == iota((size, size), 1)
    for tile in range(tiles):
        row = jnp.sum(shift[tile], axis=1, keepdims=True)
        amat[tile] += jnp.where(diagonal, size - 1.0, 0.0) - row
        total = jnp.sum(right[tile], axis=0, keepdims=True)
        rhs[tile] = total - jnp.sum(offset[tile], axis=1, keepdims=True)


def lane_copy(value, lane):
    return jnp.broadcast_to(value[:, lane : lane + 1], (8, LANES))


def row_copy(value, row):
    return jnp.broadcast_to(value[row : row + 1, :], (8, LANES))


def eliminate(amat, tile, line, solved):
    size = amat.shape[1]
    ngroup = PANEL // 8
    halves = size // LANES
    sub = iota((8, LANES), 0)
    lane = iota((8, LANES), 1)
    line = [line[:, LANES * h : LANES * h + LANES] for h in range(halves)]
    reduced = []
    for base in range(0, size, PANEL):
        first = base // LANES
        within = base % LANES
        live = range(first, halves)
        old = {
            h: amat[tile, base : base + PANEL, LANES * h : LANES * h + LANES] for h in live
        }
        part = {h: [old[h][8 * g : 8 * g + 8, :] for g in range(ngroup)] for h in live}
        right = [
            jnp.broadcast_to(
                jnp.sum(
                    jnp.where(lane - sub == within + 8 * g, line[first], 0.0), axis=1, keepdims=True
                ),
                (8, LANES),
            )
            for g in range(ngroup)
        ]
        before = list(right)
        for block in range(ngroup):
            cols = [
                [lane_copy(part[first][g], within + 8 * block + c) for c in range(8)]
                for g in range(ngroup)
            ]
            own = cols[block]
            for j in range(8):
                inverse = 1.0 / row_copy(own[j], j)
                here = sub == j
                scale = jnp.where(here, inverse, -(own[j] * inverse))

                def step(value):
                    return jnp.where(here, 0.0, value) + scale * row_copy(value, j)

                for c in range(j + 1, 8):
                    own[c] = step(own[c])
                for h in live:
                    part[h][block] = step(part[h][block])
                right[block] = step(right[block])
                yield
            for c in range(8):
                lines = {h: row_copy(part[h][block], c) for h in live}
                entry = row_copy(right[block], c)
                for g in range(ngroup):
                    if g != block:
                        for h in live:
                            part[h][g] = part[h][g] - cols[g][c] * lines[h]
                        right[g] = right[g] - cols[g][c] * entry
            yield
        reduced.append(right)
        new = {h: jnp.concatenate(part[h], axis=0) for h in live}
        for h in live:
            amat[tile, base : base + PANEL, LANES * h : LANES * h + LANES] = new[h]
        after = base + PANEL
        if after < size:
            given = jnp.concatenate(before, axis=0)
            for h in live:
                line[h] = line[h] - jnp.sum(new[h] * given, axis=0, keepdims=True)
            use = range(after // LANES, halves)
            start = use[0] * LANES
            update = dot_tn_six(
                jnp.concatenate([old[h] for h in use], axis=1),
                jnp.concatenate([new[h] for h in use], axis=1),
            )
            amat[tile, after:, start:] -= update[after - start :, :]
            yield
    solution_line = [jnp.zeros((1, LANES), F32) for _ in range(halves)]
    for base in reversed(range(0, size, PANEL)):
        first = base // LANES
        within = base % LANES
        right = reduced[base // PANEL]
        if base + PANEL < size:
            total = None
            for h in range((base + PANEL) // LANES, halves):
                term = amat[tile, base : base + PANEL, LANES * h : LANES * h + LANES] * solution_line[h]
                total = term if total is None else total + term
            known = jnp.sum(total, axis=1, keepdims=True)
            right = [right[g] - known[8 * g : 8 * g + 8, :] for g in range(ngroup)]
        placed = None
        for g in range(ngroup):
            term = jnp.where(lane - sub == within + 8 * g, right[g], 0.0)
            placed = term if placed is None else placed + term
        solution_line[first] = solution_line[first] + jnp.sum(placed, axis=0, keepdims=True)
        yield
    solved[tile] = jnp.concatenate(solution_line, axis=1)


def newton_schulz(tile, mmat, scale, zmat):
    size = mmat.shape[0]
    diagonal = iota((size, size), 0) == iota((size, size), 1)
    y = mmat / scale
    z = None
    for step in range(ITERS):
        product = y if z is None else dot_three(z, y)
        yield
        middle = jnp.where(diagonal, 1.5, 0.0) - 0.5 * product
        if step < ITERS - 1:
            y = dot_three(y, middle)
            yield
        z = middle if z is None else dot_three(middle, z)
        yield
    zmat[tile] = z * lax.rsqrt(scale)


def solve_kernel(own_ref, other_ref, w_ref, out_ref, amat, rhs, zmat):
    tiles, size = amat.shape[0], amat.shape[1]
    gram((own_ref, other_ref), w_ref, amat, rhs)
    solving, taking = [], []
    for tile in range(tiles):
        mmat = amat[tile] * (1.0 / (size - 1.0))
        squares = jnp.sum(mmat * mmat, axis=0, keepdims=True)
        scale = jnp.sqrt(jnp.sum(squares, axis=1, keepdims=True))
        taking.append(newton_schulz(tile, mmat, scale, zmat))
        solving.append(eliminate(amat, tile, rhs[tile], rhs))
    for work in taking:
        next(work)
    count = 0
    while solving or taking:
        solving = [work for work in solving if next(work, True) is None]
        if count % 12 == 0 or not solving:
            taking = [work for work in taking if next(work, True) is None]
        count += 1
    for tile in range(tiles):
        out_ref[tile] = (zmat[tile] + rhs[tile]).astype(BF16)


def apply_kernel(x_ref, w_ref, out_ref):
    size, columns = x_ref.shape
    tiles = w_ref.shape[0]
    block = 512
    each = columns // tiles // block
    for step in range(columns // block):
        at = slice(step * block, (step + 1) * block)
        xfull = x_ref[:, at].astype(F32)
        xbar = jnp.sum(xfull, axis=0, keepdims=True) * (1.0 / size)
        xpert = (xfull - xbar).astype(BF16)
        moved = jnp.dot(w_ref[step // each], xpert, preferred_element_type=F32)
        out_ref[:, at] = (xbar + moved).astype(BF16)


VMEM = pl.BlockSpec(memory_space=pltpu.VMEM)
SMEM = pl.BlockSpec(memory_space=pltpu.SMEM)


def windows(before, prior, after, groups, half):
    return pl.pallas_call(
        window_kernel,
        out_shape=jax.ShapeDtypeStruct((groups, prior.shape[0], half), BF16),
        in_specs=[VMEM] * 3,
        out_specs=VMEM,
        compiler_params=pltpu.CompilerParams(vmem_limit_bytes=4 << 20),
        name="windows",
    )(before, prior, after)


def tile_weights(here, counts, slots, before, values, rinv, after, tiles, width):
    members = before.shape[0] - 2
    return pl.pallas_call(
        functools.partial(weight_kernel, members),
        out_shape=jax.ShapeDtypeStruct((tiles + 1, width), F32),
        in_specs=[SMEM, SMEM] + [VMEM] * 5,
        out_specs=VMEM,
        scratch_shapes=[pltpu.VMEM((8, values.shape[1] + 2 * RIM), F32)],
        compiler_params=pltpu.CompilerParams(vmem_limit_bytes=8 << 20),
        cost_estimate=pl.CostEstimate(flops=50_000_000, bytes_accessed=1 << 20, transcendentals=0),
        name="tile_weights",
    )(here, counts, slots, before, values, rinv, after)


def tile_transform(own, other, sides):
    size, tiles = own.shape[0], sides.shape[0] - 1
    square = pltpu.VMEM((tiles, size, size), F32)
    return pl.pallas_call(
        solve_kernel,
        out_shape=jax.ShapeDtypeStruct((tiles, size, size), BF16),
        in_specs=[VMEM] * 3,
        out_specs=VMEM,
        scratch_shapes=[square, pltpu.VMEM((tiles, 1, size), F32), square],
        compiler_params=pltpu.CompilerParams(vmem_limit_bytes=32 << 20),
        cost_estimate=pl.CostEstimate(
            flops=2 * 9 * tiles * size * size * size * 6, bytes_accessed=8 << 20, transcendentals=0
        ),
        name="tile_transform",
    )(own, other, sides)


def tile_apply(states, transform):
    size, columns = states.shape
    return pl.pallas_call(
        apply_kernel,
        out_shape=jax.ShapeDtypeStruct((size, columns), BF16),
        in_specs=[VMEM, VMEM],
        out_specs=VMEM,
        compiler_params=pltpu.CompilerParams(vmem_limit_bytes=32 << 20),
        cost_estimate=pl.CostEstimate(
            flops=2 * size * size * columns, bytes_accessed=4 * size * columns, transcendentals=0
        ),
        name="tile_apply",
    )(states, transform)


def edges(prior, values, rinv):
    size = lax.axis_size("region")
    up = [(i, i + 1) for i in range(size - 1)]
    down = [(i + 1, i) for i in range(size - 1)]
    shape = jax.ShapeDtypeStruct((prior.shape[0] + 2, RIM), F32)
    last, first, held = pl.pallas_call(
        edge_kernel,
        out_shape=(shape, shape, jax.ShapeDtypeStruct(prior.shape, BF16)),
        in_specs=[pl.BlockSpec(memory_space=pltpu.MemorySpace.HBM)] * 3,
        out_specs=(VMEM,) * 3,
        scratch_shapes=[pltpu.SemaphoreType.DMA((5,))],
        compiler_params=pltpu.CompilerParams(vmem_limit_bytes=4 << 20),
        name="edges",
    )(prior, values, rinv)
    before = lax.ppermute(last, "region", up)
    after = lax.ppermute(first, "region", down)
    return before, held, after


def body(state_prior, obs_prior, obs_value, obs_rinv, tile_obs, tile_count):
    members_here = state_prior.shape[0]
    groups = lax.axis_size("member")
    here = lax.axis_index("member")
    tiles_region, slots = tile_obs.shape
    per_dev = tiles_region // groups
    cells = state_prior.shape[1] // tiles_region
    columns = per_dev * cells
    stride = per_dev * OBS_TILE
    half = (slots + 2 * stride) // 2

    sending = state_prior.reshape(members_here, groups, columns).transpose(1, 0, 2)

    before, held, after = edges(obs_prior, obs_value[None], obs_rinv[None])
    sent = windows(before, held, after, groups, half)
    own = lax.all_to_all(sent, "member", split_axis=0, concat_axis=0, tiled=True)
    own = own.reshape(groups * members_here, half)
    other = lax.ppermute(own, "member", [(i, i ^ 1) for i in range(groups)])
    sides = tile_weights(
        here[None], tile_count, tile_obs, before, obs_value[None], obs_rinv[None], after, per_dev, 2 * half
    )
    sending, sides = lax.optimization_barrier((sending, sides))
    states = lax.all_to_all(sending, "member", split_axis=0, concat_axis=0, tiled=True)
    states = states.reshape(groups * members_here, columns)
    transform = tile_transform(own, other, sides)
    updated = tile_apply(states, transform)
    returned = lax.all_to_all(
        updated.reshape(groups, members_here, columns),
        "member",
        split_axis=0,
        concat_axis=0,
        tiled=True,
    )
    return returned.transpose(1, 0, 2).reshape(members_here, tiles_region * cells)


def solution(mesh):
    placed = (
        P("member", "region"),
        P("member", "region"),
        P("region"),
        P("region"),
        P("region", None),
        P("region"),
    )
    return jax.shard_map(
        body, mesh=mesh, in_specs=placed, out_specs=P("member", "region"), check_vma=False
    )
```

```python
import functools

import jax
import jax.numpy as jnp
from jax import lax
from jax.experimental import pallas as pl
from jax.experimental.pallas import tpu as pltpu
from jax.sharding import PartitionSpec as P

OBS_TILE = 128
ITERS = 4
RIM = 1024
LOC = 512
LANES = 128
PANEL = 32

F32 = jnp.float32
BF16 = jnp.bfloat16


def iota(shape, dim):
    return lax.broadcasted_iota(jnp.int32, shape, dim)


def dot_nt(a, b):
    return lax.dot_general(a, b, (((1,), (1,)), ((), ())), preferred_element_type=F32)


def split2(x):
    high = x.astype(BF16)
    return high, (x - high.astype(F32)).astype(BF16)


def split3(x):
    high = x.astype(BF16)
    rest = x - high.astype(F32)
    mid = rest.astype(BF16)
    return high, mid, (rest - mid.astype(F32)).astype(BF16)


def dot_three(a, b):
    ah, al = split2(a)
    bh, bl = split2(b)
    return jnp.dot(
        jnp.concatenate([ah, ah, al], axis=1),
        jnp.concatenate([bh, bl, bh], axis=0),
        preferred_element_type=F32,
    )


def dot_tn_six(a, b):
    ah, am, al = split3(a)
    bh, bm, bl = split3(b)
    left = jnp.concatenate([ah, ah, am, am, ah, al], axis=0)
    right = jnp.concatenate([bh, bm, bh, bm, bl, bh], axis=0)
    return lax.dot_general(left, right, (((0,), (0,)), ((), ())), preferred_element_type=F32)


def window_start(group, length, groups, half):
    return group // 2 * (2 * length // groups) + group % 2 * half - RIM


def window_kernel(prior_ref, out_ref):
    groups, members, half = out_ref.shape
    length = prior_ref.shape[1]
    for group in range(groups):
        start = window_start(group, length, groups, half)
        for low in (-length, 0, length):
            left, right = max(start, low), min(start + half, low + length)
            if left < right:
                out_ref[group, :, left - start : right - start] = prior_ref[:, left - low : right - low]


def weight_kernel(
    here_ref, count_ref, slot_ref, before_ref, value_ref, rinv_ref, after_ref, out_ref, wide_ref
):
    tiles = out_ref.shape[0] - 1
    width = out_ref.shape[1]
    half = width // 2
    slots = slot_ref.shape[1]
    length = value_ref.shape[1]
    for row, own in enumerate((value_ref, rinv_ref)):
        at = slice(row, row + 1)
        wide_ref[at, :RIM] = before_ref[at, :]
        wide_ref[at, RIM : RIM + length] = own[...]
        wide_ref[at, RIM + length :] = after_ref[at, :]
    here = here_ref[0]
    chip, core = lax.shift_right_logical(here, 1), lax.bitwise_and(here, 1)
    start = chip * (2 * tiles * OBS_TILE)
    shift = core * half
    own = pl.ds(pl.multiple_of(start + shift, LANES), half)
    other = pl.ds(pl.multiple_of(start + half - shift, LANES), half)
    out_ref[tiles : tiles + 1, :half] = wide_ref[0:1, own]
    out_ref[tiles : tiles + 1, half:] = wide_ref[0:1, other]
    rinv = (wide_ref[1:2, own], wide_ref[1:2, other])
    groups = width // LANES
    padded = -(-groups // 8) * 8
    for tile in range(tiles):
        place = slot_ref[pl.ds(here * tiles + tile, 1), :] - (start + shift)
        place = jnp.where(place < 0, place + width, place)
        high = lax.shift_right_logical(place, 7)
        low = lax.bitwise_and(place, LANES - 1)
        live = iota((1, slots), 1) < count_ref[here * tiles + tile]
        ones_high = jnp.where((iota((padded, slots), 0) == high) & live, 1.0, 0.0).astype(BF16)
        ones_low = jnp.where(iota((LANES, slots), 0) == low, 1.0, 0.0).astype(BF16)
        mask = dot_nt(ones_high, ones_low)
        center = RIM + core * (tiles * OBS_TILE) + tile * OBS_TILE + OBS_TILE // 2
        for group in range(groups):
            at = slice(group * LANES, (group + 1) * LANES)
            first = group * LANES // half
            begin = group * LANES - first * half
            position = iota((1, LANES), 1) + begin
            position += half - shift if first else shift
            dist = jnp.abs(position - center).astype(F32) / LOC
            out_ref[tile : tile + 1, at] = (
                mask[group : group + 1, :]
                * rinv[first][:, begin : begin + LANES]
                / (1.0 + dist * dist)
            )


def gram(y_refs, w_ref, amat, rhs):
    size, half = y_refs[0].shape
    width = w_ref.shape[1]
    tiles = amat.shape[0]
    chunk = 256
    shift = [jnp.zeros((size, LANES), F32) for _ in range(tiles)]
    right = [jnp.zeros((8, size), F32) for _ in range(tiles)]
    offset = [jnp.zeros((1, chunk), F32) for _ in range(tiles)]
    for step in range(width // chunk):
        at = slice(step * chunk, (step + 1) * chunk)
        begin = step * chunk % half
        yb = y_refs[step * chunk // half][:, begin : begin + chunk]
        yf = yb.astype(F32)
        ybar = jnp.sum(yf, axis=0, keepdims=True) * (1.0 / size)
        pert = yf - ybar
        depart = w_ref[tiles : tiles + 1, at] - ybar
        for tile in range(tiles):
            weight = w_ref[tile : tile + 1, at]
            cweighted = pert * weight
            parts = split3(cweighted)
            product = dot_nt(parts[0], yb) + (dot_nt(parts[1], yb) + dot_nt(parts[2], yb))
            if step == 0:
                amat[tile] = product
            else:
                amat[tile] += product
            scaled = cweighted * ybar
            shift[tile] += scaled[:, :LANES] + scaled[:, LANES:]
            drive = weight * depart
            rows = iota((8, chunk), 0)
            dh, dm, dl = split3(drive)
            stacked = jnp.where(
                rows == 0,
                dh.astype(F32),
                jnp.where(rows == 1, dm.astype(F32), jnp.where(rows == 2, dl.astype(F32), 0.0)),
            ).astype(BF16)
            right[tile] += dot_nt(stacked, yb)
            offset[tile] += drive * ybar
    diagonal = iota((size, size), 0) == iota((size, size), 1)
    for tile in range(tiles):
        row = jnp.sum(shift[tile], axis=1, keepdims=True)
        amat[tile] += jnp.where(diagonal, size - 1.0, 0.0) - row
        total = jnp.sum(right[tile], axis=0, keepdims=True)
        rhs[tile] = total - jnp.sum(offset[tile], axis=1, keepdims=True)


def lane_copy(value, lane):
    return jnp.broadcast_to(value[:, lane : lane + 1], (8, LANES))


def row_copy(value, row):
    return jnp.broadcast_to(value[row : row + 1, :], (8, LANES))


def eliminate(amat, tile, line, solved):
    size = amat.shape[1]
    ngroup = PANEL // 8
    halves = size // LANES
    sub = iota((8, LANES), 0)
    lane = iota((8, LANES), 1)
    line = [line[:, LANES * h : LANES * h + LANES] for h in range(halves)]
    reduced = []
    for base in range(0, size, PANEL):
        first = base // LANES
        within = base % LANES
        live = range(first, halves)
        old = {
            h: amat[tile, base : base + PANEL, LANES * h : LANES * h + LANES] for h in live
        }
        part = {h: [old[h][8 * g : 8 * g + 8, :] for g in range(ngroup)] for h in live}
        right = [
            jnp.broadcast_to(
                jnp.sum(
                    jnp.where(lane - sub == within + 8 * g, line[first], 0.0), axis=1, keepdims=True
                ),
                (8, LANES),
            )
            for g in range(ngroup)
        ]
        before = list(right)
        for block in range(ngroup):
            cols = [
                [lane_copy(part[first][g], within + 8 * block + c) for c in range(8)]
                for g in range(ngroup)
            ]
            own = cols[block]
            for j in range(8):
                inverse = 1.0 / row_copy(own[j], j)
                here = sub == j
                scale = jnp.where(here, inverse, -(own[j] * inverse))

                def step(value):
                    return jnp.where(here, 0.0, value) + scale * row_copy(value, j)

                for c in range(j + 1, 8):
                    own[c] = step(own[c])
                for h in live:
                    part[h][block] = step(part[h][block])
                right[block] = step(right[block])
                yield
            for c in range(8):
                lines = {h: row_copy(part[h][block], c) for h in live}
                entry = row_copy(right[block], c)
                for g in range(ngroup):
                    if g != block:
                        for h in live:
                            part[h][g] = part[h][g] - cols[g][c] * lines[h]
                        right[g] = right[g] - cols[g][c] * entry
            yield
        reduced.append(right)
        new = {h: jnp.concatenate(part[h], axis=0) for h in live}
        for h in live:
            amat[tile, base : base + PANEL, LANES * h : LANES * h + LANES] = new[h]
        after = base + PANEL
        if after < size:
            given = jnp.concatenate(before, axis=0)
            for h in live:
                line[h] = line[h] - jnp.sum(new[h] * given, axis=0, keepdims=True)
            use = range(after // LANES, halves)
            start = use[0] * LANES
            update = dot_tn_six(
                jnp.concatenate([old[h] for h in use], axis=1),
                jnp.concatenate([new[h] for h in use], axis=1),
            )
            amat[tile, after:, start:] -= update[after - start :, :]
            yield
    solution_line = [jnp.zeros((1, LANES), F32) for _ in range(halves)]
    for base in reversed(range(0, size, PANEL)):
        first = base // LANES
        within = base % LANES
        right = reduced[base // PANEL]
        if base + PANEL < size:
            total = None
            for h in range((base + PANEL) // LANES, halves):
                term = amat[tile, base : base + PANEL, LANES * h : LANES * h + LANES] * solution_line[h]
                total = term if total is None else total + term
            known = jnp.sum(total, axis=1, keepdims=True)
            right = [right[g] - known[8 * g : 8 * g + 8, :] for g in range(ngroup)]
        placed = None
        for g in range(ngroup):
            term = jnp.where(lane - sub == within + 8 * g, right[g], 0.0)
            placed = term if placed is None else placed + term
        solution_line[first] = solution_line[first] + jnp.sum(placed, axis=0, keepdims=True)
        yield
    solved[tile] = jnp.concatenate(solution_line, axis=1)


def newton_schulz(tile, mmat, scale, zmat):
    size = mmat.shape[0]
    diagonal = iota((size, size), 0) == iota((size, size), 1)
    y = mmat / scale
    z = None
    for step in range(ITERS):
        product = y if z is None else dot_three(z, y)
        yield
        middle = jnp.where(diagonal, 1.5, 0.0) - 0.5 * product
        if step < ITERS - 1:
            y = dot_three(y, middle)
            yield
        z = middle if z is None else dot_three(middle, z)
        yield
    zmat[tile] = z * lax.rsqrt(scale)


def solve_kernel(own_ref, other_ref, w_ref, out_ref, amat, rhs, zmat):
    tiles, size = amat.shape[0], amat.shape[1]
    gram((own_ref, other_ref), w_ref, amat, rhs)
    solving, taking = [], []
    for tile in range(tiles):
        mmat = amat[tile] * (1.0 / (size - 1.0))
        squares = jnp.sum(mmat * mmat, axis=0, keepdims=True)
        scale = jnp.sqrt(jnp.sum(squares, axis=1, keepdims=True))
        taking.append(newton_schulz(tile, mmat, scale, zmat))
        solving.append(eliminate(amat, tile, rhs[tile], rhs))
    for work in taking:
        next(work)
    count = 0
    while solving or taking:
        solving = [work for work in solving if next(work, True) is None]
        if count % 12 == 0 or not solving:
            taking = [work for work in taking if next(work, True) is None]
        count += 1
    for tile in range(tiles):
        out_ref[tile] = (zmat[tile] + rhs[tile]).astype(BF16)


def apply_kernel(x_ref, w_ref, out_ref):
    size, columns = x_ref.shape
    tiles = w_ref.shape[0]
    block = 512
    each = columns // tiles // block
    for step in range(columns // block):
        at = slice(step * block, (step + 1) * block)
        xfull = x_ref[:, at].astype(F32)
        xbar = jnp.sum(xfull, axis=0, keepdims=True) * (1.0 / size)
        xpert = (xfull - xbar).astype(BF16)
        moved = jnp.dot(w_ref[step // each], xpert, preferred_element_type=F32)
        out_ref[:, at] = (xbar + moved).astype(BF16)


VMEM = pl.BlockSpec(memory_space=pltpu.VMEM)
SMEM = pl.BlockSpec(memory_space=pltpu.SMEM)


def windows(prior, groups, half):
    return pl.pallas_call(
        window_kernel,
        out_shape=jax.ShapeDtypeStruct((groups, prior.shape[0], half), BF16),
        in_specs=[VMEM],
        out_specs=VMEM,
        compiler_params=pltpu.CompilerParams(vmem_limit_bytes=4 << 20),
        name="windows",
    )(prior)


def tile_weights(here, counts, slots, before, values, rinv, after, tiles, width):
    return pl.pallas_call(
        weight_kernel,
        out_shape=jax.ShapeDtypeStruct((tiles + 1, width), F32),
        in_specs=[SMEM, SMEM] + [VMEM] * 5,
        out_specs=VMEM,
        scratch_shapes=[pltpu.VMEM((8, values.shape[1] + 2 * RIM), F32)],
        compiler_params=pltpu.CompilerParams(vmem_limit_bytes=8 << 20),
        cost_estimate=pl.CostEstimate(flops=50_000_000, bytes_accessed=1 << 20, transcendentals=0),
        name="tile_weights",
    )(here, counts, slots, before, values, rinv, after)


def tile_transform(own, other, sides):
    size, tiles = own.shape[0], sides.shape[0] - 1
    square = pltpu.VMEM((tiles, size, size), F32)
    return pl.pallas_call(
        solve_kernel,
        out_shape=jax.ShapeDtypeStruct((tiles, size, size), BF16),
        in_specs=[VMEM] * 3,
        out_specs=VMEM,
        scratch_shapes=[square, pltpu.VMEM((tiles, 1, size), F32), square],
        compiler_params=pltpu.CompilerParams(vmem_limit_bytes=32 << 20),
        cost_estimate=pl.CostEstimate(
            flops=2 * 9 * tiles * size * size * size * 6, bytes_accessed=8 << 20, transcendentals=0
        ),
        name="tile_transform",
    )(own, other, sides)


def tile_apply(states, transform):
    size, columns = states.shape
    return pl.pallas_call(
        apply_kernel,
        out_shape=jax.ShapeDtypeStruct((size, columns), BF16),
        in_specs=[VMEM, VMEM],
        out_specs=VMEM,
        compiler_params=pltpu.CompilerParams(vmem_limit_bytes=32 << 20),
        cost_estimate=pl.CostEstimate(
            flops=2 * size * size * columns, bytes_accessed=4 * size * columns, transcendentals=0
        ),
        name="tile_apply",
    )(states, transform)


def edges(values):
    size = lax.axis_size("region")
    up = [(i, i + 1) for i in range(size - 1)]
    down = [(i + 1, i) for i in range(size - 1)]
    length = values.shape[1]
    before = lax.ppermute(values[:, length - RIM :], "region", up)
    after = lax.ppermute(values[:, :RIM], "region", down)
    return before, after


def repaired(own, here, length, groups):
    half = own.shape[1]
    regions = lax.axis_size("region")
    pairs = []
    for group in range(groups):
        start = window_start(group, length, groups, half)
        if start < 0:
            pairs += [(group * regions + r, group * regions + r + 1) for r in range(regions - 1)]
        elif start + half > length:
            pairs += [(group * regions + r + 1, group * regions + r) for r in range(regions - 1)]
    got = lax.ppermute(own, ("member", "region"), pairs)
    place = window_start(here, length, groups, half) + jnp.arange(half)
    return jnp.where((place >= 0) & (place < length), own, got)


def body(state_prior, obs_prior, obs_value, obs_rinv, tile_obs, tile_count):
    members_here = state_prior.shape[0]
    groups = lax.axis_size("member")
    here = lax.axis_index("member")
    tiles_region, slots = tile_obs.shape
    per_dev = tiles_region // groups
    cells = state_prior.shape[1] // tiles_region
    columns = per_dev * cells
    stride = per_dev * OBS_TILE
    half = (slots + 2 * stride) // 2

    sending = state_prior.reshape(members_here, groups, columns).transpose(1, 0, 2)

    before, after = edges(jnp.stack([obs_value, obs_rinv]))
    sent = windows(obs_prior, groups, half)
    own = lax.all_to_all(sent, "member", split_axis=0, concat_axis=0, tiled=True)
    own = own.reshape(groups * members_here, half)
    sides = tile_weights(
        here[None], tile_count, tile_obs, before, obs_value[None], obs_rinv[None], after, per_dev, 2 * half
    )
    sending, own, sides = lax.optimization_barrier((sending, own, sides))
    own = repaired(own, here, obs_prior.shape[1], groups)
    other = lax.ppermute(own, "member", [(i, i ^ 1) for i in range(groups)])
    states = lax.all_to_all(sending, "member", split_axis=0, concat_axis=0, tiled=True)
    states = states.reshape(groups * members_here, columns)
    transform = tile_transform(own, other, sides)
    updated = tile_apply(states, transform)
    returned = lax.all_to_all(
        updated.reshape(groups, members_here, columns),
        "member",
        split_axis=0,
        concat_axis=0,
        tiled=True,
    )
    return returned.transpose(1, 0, 2).reshape(members_here, tiles_region * cells)


def solution(mesh):
    placed = (
        P("member", "region"),
        P("member", "region"),
        P("region"),
        P("region"),
        P("region", None),
        P("region"),
    )
    return jax.shard_map(
        body, mesh=mesh, in_specs=placed, out_specs=P("member", "region"), check_vma=False
    )
```

```python
import functools

import jax
import jax.numpy as jnp
from jax import lax
from jax.experimental import pallas as pl
from jax.experimental.pallas import tpu as pltpu
from jax.sharding import PartitionSpec as P

OBS_TILE = 128
ITERS = 4
RIM = 1024
LOC = 512
LANES = 128
PANEL = 32

F32 = jnp.float32
BF16 = jnp.bfloat16


def iota(shape, dim):
    return lax.broadcasted_iota(jnp.int32, shape, dim)


def dot_nt(a, b):
    return lax.dot_general(a, b, (((1,), (1,)), ((), ())), preferred_element_type=F32)


def split2(x):
    high = x.astype(BF16)
    return high, (x - high.astype(F32)).astype(BF16)


def split3(x):
    high = x.astype(BF16)
    rest = x - high.astype(F32)
    mid = rest.astype(BF16)
    return high, mid, (rest - mid.astype(F32)).astype(BF16)


def dot_three(a, b):
    ah, al = split2(a)
    bh, bl = split2(b)
    return jnp.dot(
        jnp.concatenate([ah, ah, al], axis=1),
        jnp.concatenate([bh, bl, bh], axis=0),
        preferred_element_type=F32,
    )


def dot_tn_six(a, b):
    ah, am, al = split3(a)
    bh, bm, bl = split3(b)
    left = jnp.concatenate([ah, ah, am, am, ah, al], axis=0)
    right = jnp.concatenate([bh, bm, bh, bm, bl, bh], axis=0)
    return lax.dot_general(left, right, (((0,), (0,)), ((), ())), preferred_element_type=F32)


def window_start(group, length, groups, half):
    return group // 2 * (2 * length // groups) + group % 2 * half - RIM


def window_pieces(length, groups, half):
    pieces = []
    for group in range(groups):
        start = window_start(group, length, groups, half)
        for low in (-length, 0, length):
            left, right = max(start, low), min(start + half, low + length)
            if left < right:
                pieces.append((group, left - low, left - start, right - left))
    return pieces


def window_kernel(prior_ref, out_ref, sems):
    groups, _, half = out_ref.shape
    copies = [
        pltpu.make_async_copy(
            prior_ref.at[:, source : source + width],
            out_ref.at[group, :, target : target + width],
            sems.at[i],
        )
        for i, (group, source, target, width) in enumerate(
            window_pieces(prior_ref.shape[1], groups, half)
        )
    ]
    for copy in copies:
        copy.start()
    for copy in copies:
        copy.wait()


def weight_kernel(
    here_ref, count_ref, slot_ref, before_ref, value_ref, rinv_ref, after_ref, out_ref, wide_ref
):
    tiles = out_ref.shape[0] - 1
    width = out_ref.shape[1]
    half = width // 2
    slots = slot_ref.shape[1]
    length = value_ref.shape[1]
    for row, own in enumerate((value_ref, rinv_ref)):
        at = slice(row, row + 1)
        wide_ref[at, :RIM] = before_ref[at, :]
        wide_ref[at, RIM : RIM + length] = own[...]
        wide_ref[at, RIM + length :] = after_ref[at, :]
    here = here_ref[0]
    chip, core = lax.shift_right_logical(here, 1), lax.bitwise_and(here, 1)
    start = chip * (2 * tiles * OBS_TILE)
    shift = core * half
    own = pl.ds(pl.multiple_of(start + shift, LANES), half)
    other = pl.ds(pl.multiple_of(start + half - shift, LANES), half)
    out_ref[tiles : tiles + 1, :half] = wide_ref[0:1, own]
    out_ref[tiles : tiles + 1, half:] = wide_ref[0:1, other]
    rinv = (wide_ref[1:2, own], wide_ref[1:2, other])
    groups = width // LANES
    padded = -(-groups // 8) * 8
    for tile in range(tiles):
        place = slot_ref[pl.ds(here * tiles + tile, 1), :] - (start + shift)
        place = jnp.where(place < 0, place + width, place)
        high = lax.shift_right_logical(place, 7)
        low = lax.bitwise_and(place, LANES - 1)
        live = iota((1, slots), 1) < count_ref[here * tiles + tile]
        ones_high = jnp.where((iota((padded, slots), 0) == high) & live, 1.0, 0.0).astype(BF16)
        ones_low = jnp.where(iota((LANES, slots), 0) == low, 1.0, 0.0).astype(BF16)
        mask = dot_nt(ones_high, ones_low)
        center = RIM + core * (tiles * OBS_TILE) + tile * OBS_TILE + OBS_TILE // 2
        for group in range(groups):
            at = slice(group * LANES, (group + 1) * LANES)
            first = group * LANES // half
            begin = group * LANES - first * half
            position = iota((1, LANES), 1) + begin
            position += half - shift if first else shift
            dist = jnp.abs(position - center).astype(F32) / LOC
            out_ref[tile : tile + 1, at] = (
                mask[group : group + 1, :]
                * rinv[first][:, begin : begin + LANES]
                / (1.0 + dist * dist)
            )


def gram(y_refs, w_ref, amat, rhs):
    size, half = y_refs[0].shape
    width = w_ref.shape[1]
    tiles = amat.shape[0]
    chunk = 256
    shift = [jnp.zeros((size, LANES), F32) for _ in range(tiles)]
    right = [jnp.zeros((8, size), F32) for _ in range(tiles)]
    offset = [jnp.zeros((1, chunk), F32) for _ in range(tiles)]
    for step in range(width // chunk):
        at = slice(step * chunk, (step + 1) * chunk)
        begin = step * chunk % half
        yb = y_refs[step * chunk // half][:, begin : begin + chunk]
        yrep = jnp.concatenate([yb] * 3, axis=1)
        yf = yb.astype(F32)
        ybar = jnp.sum(yf, axis=0, keepdims=True) * (1.0 / size)
        pert = yf - ybar
        depart = w_ref[tiles : tiles + 1, at] - ybar
        for tile in range(tiles):
            weight = w_ref[tile : tile + 1, at]
            cweighted = pert * weight
            parts = split3(cweighted)
            product = dot_nt(jnp.concatenate(parts, axis=1), yrep)
            if step == 0:
                amat[tile] = product
            else:
                amat[tile] += product
            scaled = cweighted * ybar
            for begin in range(0, chunk, LANES):
                shift[tile] += scaled[:, begin : begin + LANES]
            drive = weight * depart
            rows = iota((8, chunk), 0)
            dh, dm, dl = split3(drive)
            stacked = jnp.where(
                rows == 0,
                dh.astype(F32),
                jnp.where(rows == 1, dm.astype(F32), jnp.where(rows == 2, dl.astype(F32), 0.0)),
            ).astype(BF16)
            right[tile] += dot_nt(stacked, yb)
            offset[tile] += drive * ybar
    diagonal = iota((size, size), 0) == iota((size, size), 1)
    for tile in range(tiles):
        row = jnp.sum(shift[tile], axis=1, keepdims=True)
        amat[tile] += jnp.where(diagonal, size - 1.0, 0.0) - row
        total = jnp.sum(right[tile], axis=0, keepdims=True)
        rhs[tile] = total - jnp.sum(offset[tile], axis=1, keepdims=True)


def lane_copy(value, lane):
    return jnp.broadcast_to(value[:, lane : lane + 1], (8, LANES))


def row_copy(value, row):
    return jnp.broadcast_to(value[row : row + 1, :], (8, LANES))


def eliminate(amat, tile, line, solved):
    size = amat.shape[1]
    ngroup = PANEL // 8
    halves = size // LANES
    sub = iota((8, LANES), 0)
    lane = iota((8, LANES), 1)
    line = [line[:, LANES * h : LANES * h + LANES] for h in range(halves)]
    reduced = []
    for base in range(0, size, PANEL):
        first = base // LANES
        within = base % LANES
        live = range(first, halves)
        old = {
            h: amat[tile, base : base + PANEL, LANES * h : LANES * h + LANES] for h in live
        }
        part = {h: [old[h][8 * g : 8 * g + 8, :] for g in range(ngroup)] for h in live}
        right = [
            jnp.broadcast_to(
                jnp.sum(
                    jnp.where(lane - sub == within + 8 * g, line[first], 0.0), axis=1, keepdims=True
                ),
                (8, LANES),
            )
            for g in range(ngroup)
        ]
        before = list(right)
        for block in range(ngroup):
            cols = [
                [lane_copy(part[first][g], within + 8 * block + c) for c in range(8)]
                for g in range(ngroup)
            ]
            own = cols[block]
            for j in range(8):
                inverse = 1.0 / row_copy(own[j], j)
                here = sub == j
                scale = jnp.where(here, inverse, -(own[j] * inverse))

                def step(value):
                    return jnp.where(here, 0.0, value) + scale * row_copy(value, j)

                for c in range(j + 1, 8):
                    own[c] = step(own[c])
                for h in live:
                    part[h][block] = step(part[h][block])
                right[block] = step(right[block])
                yield
            for c in range(8):
                lines = {h: row_copy(part[h][block], c) for h in live}
                entry = row_copy(right[block], c)
                for g in range(ngroup):
                    if g != block:
                        for h in live:
                            part[h][g] = part[h][g] - cols[g][c] * lines[h]
                        right[g] = right[g] - cols[g][c] * entry
            yield
        reduced.append(right)
        new = {h: jnp.concatenate(part[h], axis=0) for h in live}
        for h in live:
            amat[tile, base : base + PANEL, LANES * h : LANES * h + LANES] = new[h]
        after = base + PANEL
        if after < size:
            given = jnp.concatenate(before, axis=0)
            for h in live:
                line[h] = line[h] - jnp.sum(new[h] * given, axis=0, keepdims=True)
            use = range(after // LANES, halves)
            start = use[0] * LANES
            update = dot_tn_six(
                jnp.concatenate([old[h] for h in use], axis=1),
                jnp.concatenate([new[h] for h in use], axis=1),
            )
            amat[tile, after:, start:] -= update[after - start :, :]
            yield
    solution_line = [jnp.zeros((1, LANES), F32) for _ in range(halves)]
    for base in reversed(range(0, size, PANEL)):
        first = base // LANES
        within = base % LANES
        right = reduced[base // PANEL]
        if base + PANEL < size:
            total = None
            for h in range((base + PANEL) // LANES, halves):
                term = amat[tile, base : base + PANEL, LANES * h : LANES * h + LANES] * solution_line[h]
                total = term if total is None else total + term
            known = jnp.sum(total, axis=1, keepdims=True)
            right = [right[g] - known[8 * g : 8 * g + 8, :] for g in range(ngroup)]
        placed = None
        for g in range(ngroup):
            term = jnp.where(lane - sub == within + 8 * g, right[g], 0.0)
            placed = term if placed is None else placed + term
        solution_line[first] = solution_line[first] + jnp.sum(placed, axis=0, keepdims=True)
        yield
    solved[tile] = jnp.concatenate(solution_line, axis=1)


def newton_schulz(tile, mmat, scale, zmat):
    size = mmat.shape[0]
    diagonal = iota((size, size), 0) == iota((size, size), 1)
    y = mmat / scale
    z = None
    for step in range(ITERS):
        product = y if z is None else dot_three(z, y)
        yield
        middle = jnp.where(diagonal, 1.5, 0.0) - 0.5 * product
        if step < ITERS - 1:
            y = dot_three(y, middle)
            yield
        z = middle if z is None else dot_three(middle, z)
        yield
    zmat[tile] = z * lax.rsqrt(scale)


def solve_kernel(own_ref, other_ref, w_ref, out_ref, amat, rhs, zmat):
    tiles, size = amat.shape[0], amat.shape[1]
    gram((own_ref, other_ref), w_ref, amat, rhs)
    solving, taking = [], []
    for tile in range(tiles):
        mmat = amat[tile] * (1.0 / (size - 1.0))
        squares = jnp.sum(mmat * mmat, axis=0, keepdims=True)
        scale = jnp.sqrt(jnp.sum(squares, axis=1, keepdims=True))
        taking.append(newton_schulz(tile, mmat, scale, zmat))
        solving.append(eliminate(amat, tile, rhs[tile], rhs))
    for work in taking:
        next(work)
    count = 0
    while solving or taking:
        solving = [work for work in solving if next(work, True) is None]
        if count % 12 == 0 or not solving:
            taking = [work for work in taking if next(work, True) is None]
        count += 1
    for tile in range(tiles):
        out_ref[tile] = (zmat[tile] + rhs[tile]).astype(BF16)


def apply_kernel(x_ref, w_ref, out_ref):
    size, columns = x_ref.shape
    tiles = w_ref.shape[0]
    block = 512
    each = columns // tiles // block
    for step in range(columns // block):
        at = slice(step * block, (step + 1) * block)
        xfull = x_ref[:, at].astype(F32)
        xbar = jnp.sum(xfull, axis=0, keepdims=True) * (1.0 / size)
        xpert = (xfull - xbar).astype(BF16)
        moved = jnp.dot(w_ref[step // each], xpert, preferred_element_type=F32)
        out_ref[:, at] = (xbar + moved).astype(BF16)


VMEM = pl.BlockSpec(memory_space=pltpu.VMEM)
SMEM = pl.BlockSpec(memory_space=pltpu.SMEM)


def windows(prior, groups, half):
    count = len(window_pieces(prior.shape[1], groups, half))
    hbm = pl.BlockSpec(memory_space=pl.ANY)
    return pl.pallas_call(
        window_kernel,
        out_shape=jax.ShapeDtypeStruct((groups, prior.shape[0], half), BF16),
        in_specs=[hbm],
        out_specs=hbm,
        scratch_shapes=[pltpu.SemaphoreType.DMA((count,))],
        name="windows",
    )(prior)


def tile_weights(here, counts, slots, before, values, rinv, after, tiles, width):
    return pl.pallas_call(
        weight_kernel,
        out_shape=jax.ShapeDtypeStruct((tiles + 1, width), F32),
        in_specs=[SMEM, SMEM] + [VMEM] * 5,
        out_specs=VMEM,
        scratch_shapes=[pltpu.VMEM((8, values.shape[1] + 2 * RIM), F32)],
        compiler_params=pltpu.CompilerParams(vmem_limit_bytes=8 << 20),
        cost_estimate=pl.CostEstimate(flops=50_000_000, bytes_accessed=1 << 20, transcendentals=0),
        name="tile_weights",
    )(here, counts, slots, before, values, rinv, after)


def tile_transform(own, other, sides):
    size, tiles = own.shape[0], sides.shape[0] - 1
    square = pltpu.VMEM((tiles, size, size), F32)
    return pl.pallas_call(
        solve_kernel,
        out_shape=jax.ShapeDtypeStruct((tiles, size, size), BF16),
        in_specs=[VMEM] * 3,
        out_specs=VMEM,
        scratch_shapes=[square, pltpu.VMEM((tiles, 1, size), F32), square],
        compiler_params=pltpu.CompilerParams(vmem_limit_bytes=32 << 20),
        cost_estimate=pl.CostEstimate(
            flops=2 * 9 * tiles * size * size * size * 6, bytes_accessed=8 << 20, transcendentals=0
        ),
        name="tile_transform",
    )(own, other, sides)


def tile_apply(states, transform):
    size, columns = states.shape
    return pl.pallas_call(
        apply_kernel,
        out_shape=jax.ShapeDtypeStruct((size, columns), BF16),
        in_specs=[VMEM, VMEM],
        out_specs=VMEM,
        compiler_params=pltpu.CompilerParams(vmem_limit_bytes=32 << 20),
        cost_estimate=pl.CostEstimate(
            flops=2 * size * size * columns, bytes_accessed=4 * size * columns, transcendentals=0
        ),
        name="tile_apply",
    )(states, transform)


def edges(values):
    size = lax.axis_size("region")
    up = [(i, i + 1) for i in range(size - 1)]
    down = [(i + 1, i) for i in range(size - 1)]
    length = values.shape[1]
    before = lax.ppermute(values[:, length - RIM :], "region", up)
    after = lax.ppermute(values[:, :RIM], "region", down)
    return before, after


def repaired(own, here, length, groups):
    half = own.shape[1]
    regions = lax.axis_size("region")
    pairs = []
    for group in range(groups):
        start = window_start(group, length, groups, half)
        if start < 0:
            pairs += [(group * regions + r, group * regions + r + 1) for r in range(regions - 1)]
        elif start + half > length:
            pairs += [(group * regions + r + 1, group * regions + r) for r in range(regions - 1)]
    got = lax.ppermute(own, ("member", "region"), pairs)
    place = window_start(here, length, groups, half) + jnp.arange(half)
    return jnp.where((place >= 0) & (place < length), own, got)


def body(state_prior, obs_prior, obs_value, obs_rinv, tile_obs, tile_count):
    members_here = state_prior.shape[0]
    groups = lax.axis_size("member")
    here = lax.axis_index("member")
    tiles_region, slots = tile_obs.shape
    per_dev = tiles_region // groups
    cells = state_prior.shape[1] // tiles_region
    columns = per_dev * cells
    stride = per_dev * OBS_TILE
    half = (slots + 2 * stride) // 2

    sending = state_prior.reshape(members_here, groups, columns).transpose(1, 0, 2)

    before, after = edges(jnp.stack([obs_value, obs_rinv]))
    sent = windows(obs_prior, groups, half)
    own = lax.all_to_all(sent, "member", split_axis=0, concat_axis=0, tiled=True)
    own = own.reshape(groups * members_here, half)
    sides = tile_weights(
        here[None], tile_count, tile_obs, before, obs_value[None], obs_rinv[None], after, per_dev, 2 * half
    )
    sending, own, sides = lax.optimization_barrier((sending, own, sides))
    own = repaired(own, here, obs_prior.shape[1], groups)
    other = lax.ppermute(own, "member", [(i, i ^ 1) for i in range(groups)])
    states = lax.all_to_all(sending, "member", split_axis=0, concat_axis=0, tiled=True)
    states = states.reshape(groups * members_here, columns)
    transform = tile_transform(own, other, sides)
    updated = tile_apply(states, transform)
    returned = lax.all_to_all(
        updated.reshape(groups, members_here, columns),
        "member",
        split_axis=0,
        concat_axis=0,
        tiled=True,
    )
    return returned.transpose(1, 0, 2).reshape(members_here, tiles_region * cells)


def solution(mesh):
    placed = (
        P("member", "region"),
        P("member", "region"),
        P("region"),
        P("region"),
        P("region", None),
        P("region"),
    )
    return jax.shard_map(
        body, mesh=mesh, in_specs=placed, out_specs=P("member", "region"), check_vma=False
    )
```

```python
import functools

import jax
import jax.numpy as jnp
from jax import lax
from jax.experimental import pallas as pl
from jax.experimental.pallas import tpu as pltpu
from jax.sharding import PartitionSpec as P

OBS_TILE = 128
ITERS = 4
RIM = 1024
LOC = 512
LANES = 128
PANEL = 32

F32 = jnp.float32
BF16 = jnp.bfloat16


def iota(shape, dim):
    return lax.broadcasted_iota(jnp.int32, shape, dim)


def dot_nt(a, b):
    return lax.dot_general(a, b, (((1,), (1,)), ((), ())), preferred_element_type=F32)


def split2(x):
    high = x.astype(BF16)
    return high, (x - high.astype(F32)).astype(BF16)


def split3(x):
    high = x.astype(BF16)
    rest = x - high.astype(F32)
    mid = rest.astype(BF16)
    return high, mid, (rest - mid.astype(F32)).astype(BF16)


def dot_three(a, b):
    ah, al = split2(a)
    bh, bl = split2(b)
    return jnp.dot(
        jnp.concatenate([ah, ah, al], axis=1),
        jnp.concatenate([bh, bl, bh], axis=0),
        preferred_element_type=F32,
    )


def dot_tn_six(a, b):
    ah, am, al = split3(a)
    bh, bm, bl = split3(b)
    left = jnp.concatenate([ah, ah, am, am, ah, al], axis=0)
    right = jnp.concatenate([bh, bm, bh, bm, bl, bh], axis=0)
    return lax.dot_general(left, right, (((0,), (0,)), ((), ())), preferred_element_type=F32)


def window_start(group, length, groups, half):
    return group // 2 * (2 * length // groups) + group % 2 * half - RIM


def window_kernel(prior_ref, out_ref, held_ref, sem):
    groups, members, half = out_ref.shape
    length = prior_ref.shape[1]
    copy = pltpu.make_async_copy(prior_ref, held_ref, sem)
    copy.start()
    copy.wait()
    for group in range(groups):
        start = window_start(group, length, groups, half)
        for low in (-length, 0, length):
            left, right = max(start, low), min(start + half, low + length)
            if left < right:
                out_ref[group, :, left - start : right - start] = held_ref[:, left - low : right - low]


def weight_kernel(
    here_ref, count_ref, slot_ref, before_ref, value_ref, rinv_ref, after_ref, out_ref, wide_ref
):
    tiles = out_ref.shape[0] - 1
    width = out_ref.shape[1]
    half = width // 2
    slots = slot_ref.shape[1]
    length = value_ref.shape[1]
    for row, own in enumerate((value_ref, rinv_ref)):
        at = slice(row, row + 1)
        wide_ref[at, :RIM] = before_ref[at, :]
        wide_ref[at, RIM : RIM + length] = own[...]
        wide_ref[at, RIM + length :] = after_ref[at, :]
    here = here_ref[0]
    chip, core = lax.shift_right_logical(here, 1), lax.bitwise_and(here, 1)
    start = chip * (2 * tiles * OBS_TILE)
    shift = core * half
    own = pl.ds(pl.multiple_of(start + shift, LANES), half)
    other = pl.ds(pl.multiple_of(start + half - shift, LANES), half)
    out_ref[tiles : tiles + 1, :half] = wide_ref[0:1, own]
    out_ref[tiles : tiles + 1, half:] = wide_ref[0:1, other]
    rinv = (wide_ref[1:2, own], wide_ref[1:2, other])
    groups = width // LANES
    padded = -(-groups // 8) * 8
    for tile in range(tiles):
        place = slot_ref[pl.ds(here * tiles + tile, 1), :] - (start + shift)
        place = jnp.where(place < 0, place + width, place)
        high = lax.shift_right_logical(place, 7)
        low = lax.bitwise_and(place, LANES - 1)
        live = iota((1, slots), 1) < count_ref[here * tiles + tile]
        ones_high = jnp.where((iota((padded, slots), 0) == high) & live, 1.0, 0.0).astype(BF16)
        ones_low = jnp.where(iota((LANES, slots), 0) == low, 1.0, 0.0).astype(BF16)
        mask = dot_nt(ones_high, ones_low)
        center = RIM + core * (tiles * OBS_TILE) + tile * OBS_TILE + OBS_TILE // 2
        for group in range(groups):
            at = slice(group * LANES, (group + 1) * LANES)
            first = group * LANES // half
            begin = group * LANES - first * half
            position = iota((1, LANES), 1) + begin
            position += half - shift if first else shift
            dist = jnp.abs(position - center).astype(F32) / LOC
            out_ref[tile : tile + 1, at] = (
                mask[group : group + 1, :]
                * rinv[first][:, begin : begin + LANES]
                / (1.0 + dist * dist)
            )


def gram(y_refs, w_ref, amat, rhs):
    size, half = y_refs[0].shape
    width = w_ref.shape[1]
    tiles = amat.shape[0]
    chunk = 256
    shift = [jnp.zeros((size, LANES), F32) for _ in range(tiles)]
    right = [jnp.zeros((8, size), F32) for _ in range(tiles)]
    offset = [jnp.zeros((1, chunk), F32) for _ in range(tiles)]
    for step in range(width // chunk):
        at = slice(step * chunk, (step + 1) * chunk)
        begin = step * chunk % half
        yb = y_refs[step * chunk // half][:, begin : begin + chunk]
        yrep = jnp.concatenate([yb] * 3, axis=1)
        yf = yb.astype(F32)
        ybar = jnp.sum(yf, axis=0, keepdims=True) * (1.0 / size)
        pert = yf - ybar
        depart = w_ref[tiles : tiles + 1, at] - ybar
        for tile in range(tiles):
            weight = w_ref[tile : tile + 1, at]
            cweighted = pert * weight
            parts = split3(cweighted)
            product = dot_nt(jnp.concatenate(parts, axis=1), yrep)
            if step == 0:
                amat[tile] = product
            else:
                amat[tile] += product
            scaled = cweighted * ybar
            for begin in range(0, chunk, LANES):
                shift[tile] += scaled[:, begin : begin + LANES]
            drive = weight * depart
            rows = iota((8, chunk), 0)
            dh, dm, dl = split3(drive)
            stacked = jnp.where(
                rows == 0,
                dh.astype(F32),
                jnp.where(rows == 1, dm.astype(F32), jnp.where(rows == 2, dl.astype(F32), 0.0)),
            ).astype(BF16)
            right[tile] += dot_nt(stacked, yb)
            offset[tile] += drive * ybar
    diagonal = iota((size, size), 0) == iota((size, size), 1)
    for tile in range(tiles):
        row = jnp.sum(shift[tile], axis=1, keepdims=True)
        amat[tile] += jnp.where(diagonal, size - 1.0, 0.0) - row
        total = jnp.sum(right[tile], axis=0, keepdims=True)
        rhs[tile] = total - jnp.sum(offset[tile], axis=1, keepdims=True)


def lane_copy(value, lane):
    return jnp.broadcast_to(value[:, lane : lane + 1], (8, LANES))


def row_copy(value, row):
    return jnp.broadcast_to(value[row : row + 1, :], (8, LANES))


def eliminate(amat, tile, line, solved):
    size = amat.shape[1]
    ngroup = PANEL // 8
    halves = size // LANES
    sub = iota((8, LANES), 0)
    lane = iota((8, LANES), 1)
    line = [line[:, LANES * h : LANES * h + LANES] for h in range(halves)]
    reduced = []
    for base in range(0, size, PANEL):
        first = base // LANES
        within = base % LANES
        live = range(first, halves)
        old = {
            h: amat[tile, base : base + PANEL, LANES * h : LANES * h + LANES] for h in live
        }
        part = {h: [old[h][8 * g : 8 * g + 8, :] for g in range(ngroup)] for h in live}
        right = [
            jnp.broadcast_to(
                jnp.sum(
                    jnp.where(lane - sub == within + 8 * g, line[first], 0.0), axis=1, keepdims=True
                ),
                (8, LANES),
            )
            for g in range(ngroup)
        ]
        before = list(right)
        for block in range(ngroup):
            cols = [
                [lane_copy(part[first][g], within + 8 * block + c) for c in range(8)]
                for g in range(ngroup)
            ]
            own = cols[block]
            for j in range(8):
                inverse = 1.0 / row_copy(own[j], j)
                here = sub == j
                scale = jnp.where(here, inverse, -(own[j] * inverse))

                def step(value):
                    return jnp.where(here, 0.0, value) + scale * row_copy(value, j)

                for c in range(j + 1, 8):
                    own[c] = step(own[c])
                for h in live:
                    part[h][block] = step(part[h][block])
                right[block] = step(right[block])
                yield
            for c in range(8):
                lines = {h: row_copy(part[h][block], c) for h in live}
                entry = row_copy(right[block], c)
                for g in range(ngroup):
                    if g != block:
                        for h in live:
                            part[h][g] = part[h][g] - cols[g][c] * lines[h]
                        right[g] = right[g] - cols[g][c] * entry
            yield
        reduced.append(right)
        new = {h: jnp.concatenate(part[h], axis=0) for h in live}
        for h in live:
            amat[tile, base : base + PANEL, LANES * h : LANES * h + LANES] = new[h]
        after = base + PANEL
        if after < size:
            given = jnp.concatenate(before, axis=0)
            for h in live:
                line[h] = line[h] - jnp.sum(new[h] * given, axis=0, keepdims=True)
            use = range(after // LANES, halves)
            start = use[0] * LANES
            update = dot_tn_six(
                jnp.concatenate([old[h] for h in use], axis=1),
                jnp.concatenate([new[h] for h in use], axis=1),
            )
            amat[tile, after:, start:] -= update[after - start :, :]
            yield
    solution_line = [jnp.zeros((1, LANES), F32) for _ in range(halves)]
    for base in reversed(range(0, size, PANEL)):
        first = base // LANES
        within = base % LANES
        right = reduced[base // PANEL]
        if base + PANEL < size:
            total = None
            for h in range((base + PANEL) // LANES, halves):
                term = amat[tile, base : base + PANEL, LANES * h : LANES * h + LANES] * solution_line[h]
                total = term if total is None else total + term
            known = jnp.sum(total, axis=1, keepdims=True)
            right = [right[g] - known[8 * g : 8 * g + 8, :] for g in range(ngroup)]
        placed = None
        for g in range(ngroup):
            term = jnp.where(lane - sub == within + 8 * g, right[g], 0.0)
            placed = term if placed is None else placed + term
        solution_line[first] = solution_line[first] + jnp.sum(placed, axis=0, keepdims=True)
        yield
    solved[tile] = jnp.concatenate(solution_line, axis=1)


def newton_schulz(tile, mmat, scale, zmat):
    size = mmat.shape[0]
    diagonal = iota((size, size), 0) == iota((size, size), 1)
    y = mmat / scale
    z = None
    for step in range(ITERS):
        product = y if z is None else dot_three(z, y)
        yield
        middle = jnp.where(diagonal, 1.5, 0.0) - 0.5 * product
        if step < ITERS - 1:
            y = dot_three(y, middle)
            yield
        z = middle if z is None else dot_three(middle, z)
        yield
    zmat[tile] = z * lax.rsqrt(scale)


def solve_kernel(own_ref, other_ref, w_ref, out_ref, amat, rhs, zmat):
    tiles, size = amat.shape[0], amat.shape[1]
    gram((own_ref, other_ref), w_ref, amat, rhs)
    solving, taking = [], []
    for tile in range(tiles):
        mmat = amat[tile] * (1.0 / (size - 1.0))
        squares = jnp.sum(mmat * mmat, axis=0, keepdims=True)
        scale = jnp.sqrt(jnp.sum(squares, axis=1, keepdims=True))
        taking.append(newton_schulz(tile, mmat, scale, zmat))
        solving.append(eliminate(amat, tile, rhs[tile], rhs))
    for work in taking:
        next(work)
    count = 0
    while solving or taking:
        solving = [work for work in solving if next(work, True) is None]
        if count % 12 == 0 or not solving:
            taking = [work for work in taking if next(work, True) is None]
        count += 1
    for tile in range(tiles):
        out_ref[tile] = (zmat[tile] + rhs[tile]).astype(BF16)


def apply_kernel(x_ref, w_ref, out_ref):
    size, columns = x_ref.shape
    tiles = w_ref.shape[0]
    block = 512
    each = columns // tiles // block
    for step in range(columns // block):
        at = slice(step * block, (step + 1) * block)
        xfull = x_ref[:, at].astype(F32)
        xbar = jnp.sum(xfull, axis=0, keepdims=True) * (1.0 / size)
        xpert = (xfull - xbar).astype(BF16)
        moved = jnp.dot(w_ref[step // each], xpert, preferred_element_type=F32)
        out_ref[:, at] = (xbar + moved).astype(BF16)


VMEM = pl.BlockSpec(memory_space=pltpu.VMEM)
SMEM = pl.BlockSpec(memory_space=pltpu.SMEM)


def windows(prior, groups, half):
    return pl.pallas_call(
        window_kernel,
        out_shape=jax.ShapeDtypeStruct((groups, prior.shape[0], half), BF16),
        in_specs=[pl.BlockSpec(memory_space=pl.ANY)],
        out_specs=VMEM,
        scratch_shapes=[pltpu.VMEM(prior.shape, BF16), pltpu.SemaphoreType.DMA],
        name="windows",
    )(prior)


def tile_weights(here, counts, slots, before, values, rinv, after, tiles, width):
    return pl.pallas_call(
        weight_kernel,
        out_shape=jax.ShapeDtypeStruct((tiles + 1, width), F32),
        in_specs=[SMEM, SMEM] + [VMEM] * 5,
        out_specs=VMEM,
        scratch_shapes=[pltpu.VMEM((8, values.shape[1] + 2 * RIM), F32)],
        compiler_params=pltpu.CompilerParams(vmem_limit_bytes=8 << 20),
        cost_estimate=pl.CostEstimate(flops=50_000_000, bytes_accessed=1 << 20, transcendentals=0),
        name="tile_weights",
    )(here, counts, slots, before, values, rinv, after)


def tile_transform(own, other, sides):
    size, tiles = own.shape[0], sides.shape[0] - 1
    square = pltpu.VMEM((tiles, size, size), F32)
    return pl.pallas_call(
        solve_kernel,
        out_shape=jax.ShapeDtypeStruct((tiles, size, size), BF16),
        in_specs=[VMEM] * 3,
        out_specs=VMEM,
        scratch_shapes=[square, pltpu.VMEM((tiles, 1, size), F32), square],
        compiler_params=pltpu.CompilerParams(vmem_limit_bytes=32 << 20),
        cost_estimate=pl.CostEstimate(
            flops=2 * 9 * tiles * size * size * size * 6, bytes_accessed=8 << 20, transcendentals=0
        ),
        name="tile_transform",
    )(own, other, sides)


def tile_apply(states, transform):
    size, columns = states.shape
    return pl.pallas_call(
        apply_kernel,
        out_shape=jax.ShapeDtypeStruct((size, columns), BF16),
        in_specs=[VMEM, VMEM],
        out_specs=VMEM,
        compiler_params=pltpu.CompilerParams(vmem_limit_bytes=32 << 20),
        cost_estimate=pl.CostEstimate(
            flops=2 * size * size * columns, bytes_accessed=4 * size * columns, transcendentals=0
        ),
        name="tile_apply",
    )(states, transform)


def edges(values):
    size = lax.axis_size("region")
    up = [(i, i + 1) for i in range(size - 1)]
    down = [(i + 1, i) for i in range(size - 1)]
    length = values.shape[1]
    before = lax.ppermute(values[:, length - RIM :], "region", up)
    after = lax.ppermute(values[:, :RIM], "region", down)
    return before, after


def repaired(own, here, length, groups):
    half = own.shape[1]
    regions = lax.axis_size("region")
    pairs = []
    for group in range(groups):
        start = window_start(group, length, groups, half)
        if start < 0:
            pairs += [(group * regions + r, group * regions + r + 1) for r in range(regions - 1)]
        elif start + half > length:
            pairs += [(group * regions + r + 1, group * regions + r) for r in range(regions - 1)]
    got = lax.ppermute(own, ("member", "region"), pairs)
    place = window_start(here, length, groups, half) + jnp.arange(half)
    return jnp.where((place >= 0) & (place < length), own, got)


def body(state_prior, obs_prior, obs_value, obs_rinv, tile_obs, tile_count):
    members_here = state_prior.shape[0]
    groups = lax.axis_size("member")
    here = lax.axis_index("member")
    tiles_region, slots = tile_obs.shape
    per_dev = tiles_region // groups
    cells = state_prior.shape[1] // tiles_region
    columns = per_dev * cells
    stride = per_dev * OBS_TILE
    half = (slots + 2 * stride) // 2

    sending = state_prior.reshape(members_here, groups, columns).transpose(1, 0, 2)

    before, after = edges(jnp.stack([obs_value, obs_rinv]))
    sent = windows(obs_prior, groups, half)
    own = lax.all_to_all(sent, "member", split_axis=0, concat_axis=0, tiled=True)
    own = own.reshape(groups * members_here, half)
    sides = tile_weights(
        here[None], tile_count, tile_obs, before, obs_value[None], obs_rinv[None], after, per_dev, 2 * half
    )
    sending, own, sides = lax.optimization_barrier((sending, own, sides))
    own = repaired(own, here, obs_prior.shape[1], groups)
    other = lax.ppermute(own, "member", [(i, i ^ 1) for i in range(groups)])
    states = lax.all_to_all(sending, "member", split_axis=0, concat_axis=0, tiled=True)
    states = states.reshape(groups * members_here, columns)
    transform = tile_transform(own, other, sides)
    updated = tile_apply(states, transform)
    returned = lax.all_to_all(
        updated.reshape(groups, members_here, columns),
        "member",
        split_axis=0,
        concat_axis=0,
        tiled=True,
    )
    return returned.transpose(1, 0, 2).reshape(members_here, tiles_region * cells)


def solution(mesh):
    placed = (
        P("member", "region"),
        P("member", "region"),
        P("region"),
        P("region"),
        P("region", None),
        P("region"),
    )
    return jax.shard_map(
        body, mesh=mesh, in_specs=placed, out_specs=P("member", "region"), check_vma=False
    )
```
